512 devices in a mesh: tm: 16 (over x, y_lo, core), slab: 32 (over z, y_hi).
Axes of the slice: x: 4, y: 4 (y_hi: 2, y_lo: 2; y = y_hi * 2 + y_lo), z: 16, core: 2. Of those that a mesh axis runs over, the one named last changes fastest.
Arguments:
- starts: float32 [16, 4, 256, 64, 128], P('tm', None, 'slab'), may hold values from 0 to 1
- tissue: int32 [256, 64, 128], P('slab'), may hold values 0 or 1
- fibers: int32 [256, 64, 128], P('slab'), may hold values from 0 to 3
- pacing: int32 [256, 64, 128], P('slab'), may hold values 0 or 1
- conductances: float32 [4, 3], replicated, may hold values from 0.1 to 2, as said below
Outputs:
- defect: float32 [16, 4, 256, 64, 128], P('tm', None, 'slab')
- gradient: float32 [16, 4, 256, 64, 128], P('tm', None, 'slab')
The draws below stay inside these ranges and needn't reach their ends.
Inputs may be any that keep to these rules, and one draw needn't show every extreme that they name: `conductances`: the apex-to-base column lies between 1.0 and 2.0, the two cross columns between 0.1 and 0.4.
All inputs are finite; a program needn't handle non-finite values. No bound on the sum of `tissue` or of `pacing` on one device may be relied on, other than what follows from the above.
Results may differ from the reference program's by a relative error of at most 0.00002.
Values sent between devices are 32-bit elements; how exact they have to be, the bound alone decides.
No kernel may reach another device: no remote copies, remote signals or barrier semaphores. Data moves between devices by JAX's collectives and lax.ppermute only.
A program may use at most 64 MiB of HBM per device.

```python
import math
import jax
import jax.numpy as jnp
from jax import lax

NX = 64
NY = 128
STEPS = 4
CLASSES = 4
SECTIONS = 16
NZ = 256


def draw_conductances(key, part):
    depth_key = jax.random.fold_in(key, 11)
    cross_key = jax.random.fold_in(key, 23)
    depth_values = jnp.exp(jax.random.uniform(depth_key, (CLASSES, 1), jnp.float32, math.log(1.0), math.log(2.0)))
    cross_values = jnp.exp(jax.random.uniform(cross_key, (CLASSES, 2), jnp.float32, math.log(0.1), math.log(0.4)))
    return jnp.clip(jnp.concatenate([depth_values, cross_values], axis=1), 0.1, 2.0).astype(jnp.float32)


def plant(values, rng, low, largest):
    longest = values.shape.index(max(values.shape))
    spots = []
    for shift in (0, 1):
        where = [jax.random.randint(jax.random.fold_in(rng, axis), (), 0, length) for axis, length in enumerate(values.shape)]
        where[longest] = (where[longest] + shift) % values.shape[longest]
        spots.append(tuple(where))
    return values.at[spots[0]].set(low).at[spots[1]].set(largest)


def levels(rng, extent, pieces, low, largest):
    level, own = 1.0, jax.random.fold_in(rng, 6)
    for position, shards_of in pieces:
        heights = jnp.exp(jax.random.uniform(jax.random.fold_in(own, position), (shards_of,), jnp.float32, low / len(pieces), largest / len(pieces)))
        level = level * jnp.repeat(heights, extent[position] // shards_of).reshape([-1 if axis == position else 1 for axis in range(len(extent))])
    return level


def setup_inputs(seed: int = 0) -> dict:
    arg_keys = jax.random.split(jax.random.key(seed), 6)
    starts = jnp.clip(1.0 * jax.random.uniform(arg_keys[0], (SECTIONS, 4, NZ, NX, NY), jnp.float32) ** levels(arg_keys[0], (SECTIONS, 4, NZ, NX, NY), ((0, 16), (2, 32)), -0.2, 0.2), 0.0, 1.0)
    tissue = plant((jax.random.randint(arg_keys[1], (NZ, NX, NY), 0, 8) < 7).astype(jnp.int32), jax.random.fold_in(arg_keys[1], 1), 0, 1)
    fibers = plant(jax.random.randint(arg_keys[2], (NZ, NX, NY), 0, CLASSES), jax.random.fold_in(arg_keys[2], 1), 0, CLASSES - 1).astype(jnp.int32)
    pacing = plant((jax.random.randint(arg_keys[3], (NZ, NX, NY), 0, 8) < 1).astype(jnp.int32), jax.random.fold_in(arg_keys[3], 1), 0, 1)
    conductances = draw_conductances(jax.random.fold_in(arg_keys[5], 71), 0)
    return {"starts": starts, "tissue": tissue, "fibers": fibers, "pacing": pacing, "conductances": conductances}


TIME_STEP = 0.15
FAST_GAIN = 2.0
SLOW_GAIN = 1.0
STIM_GAIN = 4.0
GATE_SLOPE = 8.0
GATE_RATES = (0.3, 0.1, 0.03)
GATE_MIDDLES = (0.2, 0.5, 0.8)

def pad_axis(operand, axis_index):
    widths = [(0, 0)] * operand.ndim
    widths[axis_index] = (1, 1)
    return jnp.pad(operand, widths)

def conductivity(fibers, conductances, axis_index):
    summed = jnp.zeros(fibers.shape, jnp.float32)
    for class_index in range(conductances.shape[0]):
        summed = summed + jnp.where(fibers == class_index, conductances[class_index, axis_index], jnp.zeros((), jnp.float32))
    return summed

def pair_weight(sigma_padded, share_padded, axis_index):
    length = sigma_padded.shape[axis_index]
    low_sigma = lax.slice_in_dim(sigma_padded, 0, length - 1, axis=axis_index)
    high_sigma = lax.slice_in_dim(sigma_padded, 1, length, axis=axis_index)
    low_share = lax.slice_in_dim(share_padded, 0, length - 1, axis=axis_index)
    high_share = lax.slice_in_dim(share_padded, 1, length, axis=axis_index)
    return TIME_STEP * 0.5 * (low_sigma + high_sigma) * low_share * high_share

def diffuse(padded_depth, weights):
    voltage = padded_depth[1:-1]
    depth_flux = weights[0] * (padded_depth[1:] - padded_depth[:-1])
    across = pad_axis(voltage, 1)
    across_flux = weights[1] * (across[:, 1:] - across[:, :-1])
    lengthwise = pad_axis(voltage, 2)
    lengthwise_flux = weights[2] * (lengthwise[:, :, 1:] - lengthwise[:, :, :-1])
    return depth_flux[1:] - depth_flux[:-1] + (across_flux[:, 1:] - across_flux[:, :-1]) + (lengthwise_flux[:, :, 1:] - lengthwise_flux[:, :, :-1])

def reaction_step(fields, stimulus):
    voltage, gate_one, gate_two, gate_three = (fields[0], fields[1], fields[2], fields[3])
    current = FAST_GAIN * gate_one * gate_two * (1.0 - voltage) - SLOW_GAIN * gate_three * voltage + stimulus
    target_one = jax.nn.sigmoid(GATE_SLOPE * (voltage - GATE_MIDDLES[0]))
    target_two = jax.nn.sigmoid(GATE_SLOPE * (GATE_MIDDLES[1] - voltage))
    target_three = jax.nn.sigmoid(GATE_SLOPE * (voltage - GATE_MIDDLES[2]))
    return jnp.stack([voltage + TIME_STEP * current, gate_one + GATE_RATES[0] * (target_one - gate_one), gate_two + GATE_RATES[1] * (target_two - gate_two), gate_three + GATE_RATES[2] * (target_three - gate_three)])

def advance(fields, stimulus, weights):
    for step_index in range(STEPS):
        reacted = reaction_step(fields, stimulus)
        fields = reacted.at[0].add(diffuse(pad_axis(fields[0], 0), weights))
    return fields

def reference(starts, tissue, fibers, pacing, conductances):
    share = tissue.astype(jnp.float32)
    weights = tuple((pair_weight(pad_axis(conductivity(fibers, conductances, axis_index), axis_index), pad_axis(share, axis_index), axis_index) for axis_index in range(3)))
    pacing_drive = STIM_GAIN * pacing.astype(jnp.float32)
    drives = [pacing_drive if section == 0 else jnp.zeros_like(pacing_drive) for section in range(SECTIONS)]
    section_ends = [advance(starts[section], drives[section], weights) for section in range(SECTIONS)]
    defects = [section_ends[(section - 1) % SECTIONS] - starts[section] for section in range(SECTIONS)]
    gradients = []
    for section in range(SECTIONS):
        stimulus = drives[section]
        pullback = jax.vjp(lambda operand: advance(operand, stimulus, weights), starts[section])[1]
        gradients.append(pullback(defects[(section + 1) % SECTIONS])[0] - defects[section])
    return (jnp.stack(defects), jnp.stack(gradients))
```

```python
import functools

import jax
import jax.numpy as jnp
from jax import lax
from jax.experimental import pallas as pl
from jax.experimental.pallas import tpu as pltpu
from jax.sharding import PartitionSpec as P

DEEP = 8
NX = 64
NY = 128
V0, P1, G1, G2, G3, Q2, Q3, FIB, TIS, WIN = range(10)
C_W01, C_WIN, C_WX, C_WY, C_D2, C_E, C_D1 = range(7)
HALF_STEP = 0.15 * 0.5


def ahead(plane, axis):
    return pltpu.roll(plane, plane.shape[axis] - 1, axis)


def behind(plane, axis):
    return pltpu.roll(plane, 1, axis)


def sigma(cond, fiber, direction):
    summed = jnp.zeros(fiber.shape, jnp.float32)
    for c in range(4):
        summed = jnp.where(fiber == c, cond[c, direction], summed)
    return summed


def cross_weight(sig, share, axis):
    place = lax.broadcasted_iota(jnp.int32, sig.shape, axis)
    inner = jnp.where(place < sig.shape[axis] - 1, HALF_STEP, 0.0)
    return inner * (sig + ahead(sig, axis)) * (share * ahead(share, axis))


def face_weight(sig_a, share_a, sig_b, share_b):
    return HALF_STEP * (sig_a + sig_b) * (share_a * share_b)


def cross(v, wx, wy):
    fx = wx * (ahead(v, 0) - v)
    fy = wy * (ahead(v, 1) - v)
    return (fx - behind(fx, 0)) + (fy - behind(fy, 1))


def reaction(v, g1, g2, g3):
    return 0.3 * (g1 * g2) * (1.0 - v) - 0.15 * g3 * v


def tanhs(v):
    return jnp.tanh(4.0 * v - 0.8), jnp.tanh(2.0 - 4.0 * v), jnp.tanh(4.0 * v - 3.2)


def gates_next(v, g1, g2, g3):
    t1, t2, t3 = tanhs(v)
    return (
        0.7 * g1 + (0.15 + 0.15 * t1),
        0.9 * g2 + (0.05 + 0.05 * t2),
        0.97 * g3 + (0.015 + 0.015 * t3),
    )


def edge_kernel(cond, flag, starts, tissue, fibers, pacing, up, down):
    for out, (b1, b2, b3, b4) in ((up, (7, 6, 5, 4)), (down, (0, 1, 2, 3))):
        share = [tissue[b].astype(jnp.float32) for b in (b1, b2, b3, b4)]
        sig0 = [sigma(cond, fibers[b], 0) for b in (b1, b2, b3, b4)]
        wz = [face_weight(sig0[i], share[i], sig0[i + 1], share[i + 1]) for i in range(3)]
        wx = [cross_weight(sigma(cond, fibers[b], 1), share[i], 0) for i, b in enumerate((b1, b2, b3))]
        wy = [cross_weight(sigma(cond, fibers[b], 2), share[i], 1) for i, b in enumerate((b1, b2, b3))]
        stim = [(0.6 * flag[0]) * pacing[b].astype(jnp.float32) for b in (b1, b2, b3)]
        v = [starts[0, 0, b] for b in (b1, b2, b3, b4)]
        g = [[starts[0, n, b] for n in (1, 2, 3)] for b in (b1, b2, b3)]

        def own_step(i):
            total = v[i] + cross(v[i], wx[i], wy[i]) + reaction(v[i], *g[i]) + stim[i]
            total = total + wz[i] * (v[i + 1] - v[i])
            return total if i == 0 else total + wz[i - 1] * (v[i - 1] - v[i])

        out[V0] = v[0]
        out[P1] = own_step(0)
        gates = gates_next(v[0], *g[0])
        for n in range(3):
            out[G1 + n] = gates[n]
        v1_b2 = own_step(1)
        v1_b3 = own_step(2)
        out[Q2] = wz[0] * v1_b2 + stim[0]
        rest = v1_b2 + cross(v1_b2, wx[1], wy[1]) + reaction(v1_b2, *gates_next(v[1], *g[1])) + stim[1]
        rest = rest + wz[1] * (v1_b3 - v1_b2) - wz[0] * v1_b2
        out[Q3] = wz[0] * rest + stim[0]
        out[FIB] = fibers[b1].astype(jnp.float32)
        out[TIS] = share[0]
        out[WIN] = wz[0]


def weight_kernel(cond, tissue, fibers, gate, wx, wy, wz):
    before = None
    for i in range(DEEP):
        share = tissue[i].astype(jnp.float32)
        sig0 = sigma(cond, fibers[i], 0)
        wx[i] = cross_weight(sigma(cond, fibers[i], 1), share, 0)
        wy[i] = cross_weight(sigma(cond, fibers[i], 2), share, 1)
        if i:
            wz[i - 1] = face_weight(*before, sig0, share)
        before = (sig0, share)


def forward_kernel(cond, flag, starts, tissue, fibers, pacing, wx, wy, wz, low, high, ends, hist, side):
    halo = []
    for n, (msg, own) in enumerate(((low, 0), (high, DEEP - 1))):
        fib, tis = msg[FIB], msg[TIS]
        w01 = face_weight(sigma(cond, fib, 0), tis, sigma(cond, fibers[own], 0), tissue[own].astype(jnp.float32))
        side[n, C_W01] = w01
        side[n, C_WIN] = msg[WIN]
        side[n, C_WX] = cross_weight(sigma(cond, fib, 1), tis, 0)
        side[n, C_WY] = cross_weight(sigma(cond, fib, 2), tis, 1)
        halo.append(msg[V0])
    old = starts.at[0]
    for step in range(4):
        new = hist.at[step] if step < 3 else ends
        below = side[0, C_W01] * (old[0, 0] - halo[0])
        first_flux = below
        for i in range(DEEP):
            v = old[0, i]
            g = [old[n, i] for n in (1, 2, 3)]
            if i < DEEP - 1:
                above = wz[i] * (old[0, i + 1] - v)
            else:
                above = side[1, C_W01] * (halo[1] - v)
                last_flux = above
            total = v + (above - below) + cross(v, wx[i], wy[i]) + reaction(v, *g)
            new[0, i] = total + (0.6 * flag[0]) * pacing[i].astype(jnp.float32)
            for n, gate in enumerate(gates_next(v, *g)):
                new[n + 1, i] = gate
            below = above
        if step < 3:
            for n, msg in enumerate((low, high)):
                inflow = first_flux if n == 0 else -last_flux
                if step == 0:
                    halo[n] = msg[P1] + inflow
                    side[n, C_D1] = halo[n]
                    continue
                v = halo[n]
                win = side[n, C_WIN]
                g = [msg[G1], msg[G2], msg[G3]]
                if step == 1:
                    extra = msg[Q2]
                else:
                    v1 = side[n, C_D1]
                    g1 = g
                    g = gates_next(v1, *g1)
                    extra = msg[Q3] + win * win * v1
                    t1, t2, t3 = tanhs(v1)
                    side[n, C_D2] = -0.3 * (g[0] * g[1]) - 0.15 * g[2]
                    side[n, C_D1] = -0.3 * (g1[0] * g1[1]) - 0.15 * g1[2]
                    side[n, C_E] = (
                        0.6 * (1.0 - t1 * t1) * (0.3 * g[1] * (1.0 - v))
                        - 0.2 * (1.0 - t2 * t2) * (0.3 * g[0] * (1.0 - v))
                        - 0.06 * (1.0 - t3 * t3) * (0.15 * v)
                    )
                total = v + cross(v, side[n, C_WX], side[n, C_WY]) + reaction(v, *g)
                halo[n] = total + (extra - win * v) + inflow
        old = new


def pull_gates(a, g, v):
    av, a1, a2, a3 = a
    rest = 0.3 * (1.0 - v) * av
    return 0.7 * a1 + g[1] * rest, 0.9 * a2 + g[0] * rest, 0.97 * a3 - 0.15 * v * av


def pull_voltage(a, g, v):
    av, a1, a2, a3 = a
    t1, t2, t3 = tanhs(v)
    total = av * (1.0 - 0.3 * (g[0] * g[1]) - 0.15 * g[2])
    total = total + 0.6 * (1.0 - t1 * t1) * a1 - 0.2 * (1.0 - t2 * t2) * a2
    return total + 0.06 * (1.0 - t3 * t3) * a3


def send_kernel(ends, following, hist, wx, wy, wz, gap, up, down):
    for n in range(4):
        for i in range(DEEP):
            gap[n, i] = ends[n, i] - following[0, n, i]
    for out, (b1, sign) in ((up, (7, -1)), (down, (0, 1))):
        layers = [b1 + sign * d for d in range(4)]
        a = [[gap[n, b] for n in range(4)] for b in layers]
        out[0] = a[0][0]
        for m in range(3):
            fields = hist.at[2 - m]
            fresh = []
            outer = None
            for d in range(3 - m):
                b = layers[d]
                v = fields[0, b]
                g = [fields[n, b] for n in (1, 2, 3)]
                face = wz[b - 1] if sign < 0 else wz[b]
                inner = face * (a[d + 1][0] - a[d][0])
                total = pull_voltage(a[d], g, v) + cross(a[d][0], wx[b], wy[b]) + inner
                if outer is not None:
                    total = total - outer
                fresh.append([total, *pull_gates(a[d], g, v)])
                outer = inner
            a = fresh
            out[m + 1] = a[0][0]


def pull_kernel(starts, hist, gap, wx, wy, wz, side, low, high, out, work):
    halo = [low[0], high[0]]
    first = [None, None]
    old = gap
    for m in range(4):
        fields = hist.at[2 - m] if m < 3 else starts.at[0]
        new = out if m == 3 else work.at[m % 2]
        below = side[0, C_W01] * (old[0, 0] - halo[0])
        first_flux = below
        for i in range(DEEP):
            a = [old[n, i] for n in range(4)]
            v = fields[0, i]
            g = [fields[n, i] for n in (1, 2, 3)]
            if i < DEEP - 1:
                above = wz[i] * (old[0, i + 1] - a[0])
            else:
                above = side[1, C_W01] * (halo[1] - a[0])
                last_flux = above
            new[0, i] = pull_voltage(a, g, v) + (above - below) + cross(a[0], wx[i], wy[i])
            for n, gate in enumerate(pull_gates(a, g, v)):
                new[n + 1, i] = gate
            below = above
        if m < 3:
            for n, msg in enumerate((low, high)):
                inflow = first_flux if n == 0 else -last_flux
                win, px, py = side[n, C_WIN], side[n, C_WX], side[n, C_WY]
                if m == 0:
                    change = inflow
                    first[n] = inflow
                elif m == 1:
                    d = first[n]
                    change = d + cross(d, px, py) + (side[n, C_D2] - win) * d + inflow
                    second = change
                else:
                    d, d1 = last[n], first[n]
                    change = d + cross(d, px, py) + (side[n, C_D1] - win) * d + inflow
                    change = change + (win * win + side[n, C_E]) * d1
                halo[n] = msg[m + 1] + change
                if n == 0:
                    changes = [change]
                else:
                    changes.append(change)
            last = changes
        old = new


VM = pl.BlockSpec(memory_space=pltpu.VMEM)
SM = pl.BlockSpec(memory_space=pltpu.SMEM)


def f32(*shape):
    return jax.ShapeDtypeStruct(shape, jnp.float32)


def call(kernel, name, ins, outs, scratch=()):
    return pl.pallas_call(
        kernel,
        name=name,
        in_specs=ins,
        out_specs=[VM] * len(outs),
        out_shape=outs,
        scratch_shapes=list(scratch),
        compiler_params=pltpu.CompilerParams(vmem_limit_bytes=48 * 1024 * 1024),
    )


def body(starts, tissue, fibers, pacing, conductances):
    plane = (NX, NY)
    slabs = lax.axis_size("slab")
    sections = lax.axis_size("tm")
    upward = [(i, i + 1) for i in range(slabs - 1)]
    downward = [(i + 1, i) for i in range(slabs - 1)]
    earlier = [((i + 1) % sections, i) for i in range(sections)]
    later = [(i, (i + 1) % sections) for i in range(sections)]
    flag = (lax.axis_index("tm") == 0).astype(jnp.float32).reshape(1)

    up, down = call(edge_kernel, "edge", [SM, SM] + [VM] * 4, [f32(10, *plane)] * 2)(
        conductances, flag, starts, tissue, fibers, pacing
    )
    low = lax.ppermute(up, "slab", upward)
    high = lax.ppermute(down, "slab", downward)
    following = lax.ppermute(starts, "tm", earlier)
    wx, wy, wz = call(
        weight_kernel,
        "weight",
        [SM, VM, VM, pl.BlockSpec(memory_space=pl.ANY)],
        [f32(DEEP, *plane), f32(DEEP, *plane), f32(DEEP - 1, *plane)],
    )(conductances, tissue, fibers, up)
    ends, hist, side = call(
        forward_kernel,
        "forward",
        [SM, SM] + [VM] * 9,
        [f32(4, DEEP, *plane), f32(3, 4, DEEP, *plane), f32(2, 7, *plane)],
    )(conductances, flag, starts, tissue, fibers, pacing, wx, wy, wz, low, high)
    gap, up, down = call(
        send_kernel,
        "send",
        [VM] * 6,
        [f32(4, DEEP, *plane), f32(4, *plane), f32(4, *plane)],
    )(ends, following, hist, wx, wy, wz)
    low = lax.ppermute(up, "slab", upward)
    high = lax.ppermute(down, "slab", downward)
    defect = lax.ppermute(gap[None], "tm", later)
    pulled = call(
        pull_kernel,
        "pull",
        [VM] * 9,
        [f32(4, DEEP, *plane)],
        [pltpu.VMEM((2, 4, DEEP, *plane), jnp.float32)],
    )(starts, hist, gap, wx, wy, wz, side, low, high)[0]
    return defect, pulled[None] - defect


def solution(mesh):
    spread = P("tm", None, "slab", None, None)
    placed = (spread, P("slab", None, None), P("slab", None, None), P("slab", None, None), P())
    return jax.shard_map(body, mesh=mesh, in_specs=placed, out_specs=(spread, spread), check_vma=False)
```

```python
import jax
import jax.numpy as jnp
from jax import lax
from jax.experimental import pallas as pl
from jax.experimental.pallas import tpu as pltpu
from jax.sharding import PartitionSpec as P

DEEP = 8
NX = 64
NY = 128
V0, P1, G1, G2, G3, Q2, Q3, FIB, TIS, WIN = range(10)
C_W01, C_WIN, C_WX, C_WY, C_D2, C_E, C_D1 = range(7)
HALF_STEP = 0.15 * 0.5


def ahead(plane, axis):
    return pltpu.roll(plane, plane.shape[axis] - 1, axis)


def behind(plane, axis):
    return pltpu.roll(plane, 1, axis)


def sigma(cond, fiber, direction):
    summed = jnp.zeros(fiber.shape, jnp.float32)
    for c in range(4):
        summed = jnp.where(fiber == c, cond[c, direction], summed)
    return summed


def cross_weight(sig, share, axis):
    place = lax.broadcasted_iota(jnp.int32, sig.shape, axis)
    inner = jnp.where(place < sig.shape[axis] - 1, HALF_STEP, 0.0)
    return inner * (sig + ahead(sig, axis)) * (share * ahead(share, axis))


def face_weight(sig_a, share_a, sig_b, share_b):
    return HALF_STEP * (sig_a + sig_b) * (share_a * share_b)


def cross(v, wx, wy):
    fx = wx * (ahead(v, 0) - v)
    fy = wy * (ahead(v, 1) - v)
    return (fx - behind(fx, 0)) + (fy - behind(fy, 1))


def reaction(v, g1, g2, g3):
    return 0.3 * (g1 * g2) * (1.0 - v) - 0.15 * g3 * v


def tanhs(v):
    return jnp.tanh(4.0 * v - 0.8), jnp.tanh(2.0 - 4.0 * v), jnp.tanh(4.0 * v - 3.2)


def gates_next(v, g1, g2, g3):
    t1, t2, t3 = tanhs(v)
    return (
        0.7 * g1 + (0.15 + 0.15 * t1),
        0.9 * g2 + (0.05 + 0.05 * t2),
        0.97 * g3 + (0.015 + 0.015 * t3),
    )


def fetch(copies, sems):
    started = [pltpu.make_async_copy(src, dst, sems.at[n]) for n, (src, dst) in enumerate(copies)]
    for copy in started:
        copy.start()
    for copy in started:
        copy.wait()


def edge_kernel(
    cond_in, flag, starts_in, tissue_in, fibers_in, pacing_in, up, down, starts, tissue, fibers, pacing, cond, sems
):
    fetch(
        [
            (starts_in.at[0], starts),
            (tissue_in, tissue),
            (fibers_in, fibers),
            (pacing_in, pacing),
            (cond_in, cond),
        ],
        sems,
    )
    for out, (b1, b2, b3, b4) in ((up, (7, 6, 5, 4)), (down, (0, 1, 2, 3))):
        share = [tissue[b].astype(jnp.float32) for b in (b1, b2, b3, b4)]
        sig0 = [sigma(cond, fibers[b], 0) for b in (b1, b2, b3, b4)]
        wz = [face_weight(sig0[i], share[i], sig0[i + 1], share[i + 1]) for i in range(3)]
        wx = [cross_weight(sigma(cond, fibers[b], 1), share[i], 0) for i, b in enumerate((b1, b2, b3))]
        wy = [cross_weight(sigma(cond, fibers[b], 2), share[i], 1) for i, b in enumerate((b1, b2, b3))]
        stim = [(0.6 * flag[0]) * pacing[b].astype(jnp.float32) for b in (b1, b2, b3)]
        v = [starts[0, b] for b in (b1, b2, b3, b4)]
        g = [[starts[n, b] for n in (1, 2, 3)] for b in (b1, b2, b3)]

        def own_step(i):
            total = v[i] + cross(v[i], wx[i], wy[i]) + reaction(v[i], *g[i]) + stim[i]
            total = total + wz[i] * (v[i + 1] - v[i])
            return total if i == 0 else total + wz[i - 1] * (v[i - 1] - v[i])

        out[V0] = v[0]
        out[P1] = own_step(0)
        gates = gates_next(v[0], *g[0])
        for n in range(3):
            out[G1 + n] = gates[n]
        v1_b2 = own_step(1)
        v1_b3 = own_step(2)
        out[Q2] = wz[0] * v1_b2 + stim[0]
        rest = v1_b2 + cross(v1_b2, wx[1], wy[1]) + reaction(v1_b2, *gates_next(v[1], *g[1])) + stim[1]
        rest = rest + wz[1] * (v1_b3 - v1_b2) - wz[0] * v1_b2
        out[Q3] = wz[0] * rest + stim[0]
        out[FIB] = fibers[b1].astype(jnp.float32)
        out[TIS] = share[0]
        out[WIN] = wz[0]


class Fields:
    def __init__(self, inner, outer, rim_voltage, rim_gate):
        self.refs = (inner, outer)
        self.rims = (rim_voltage, rim_gate)

    def plane(self, field, layer):
        rim = self.rims[0] if field == 0 else self.rims[1]
        inside = rim <= layer < DEEP - rim
        return self.refs[0 if inside else 1][field, layer]

    def all(self, layer):
        return [self.plane(n, layer) for n in range(4)]


def forward_fields(starts, inner, outer):
    return [Fields(starts, None, 0, 0)] + [Fields(inner[j - 1], outer[j - 1], j, j - 1) for j in (1, 2, 3)]


def inner_layers(rim):
    return range(rim, DEEP - rim)


def rim_layers(rim):
    return [i for i in range(DEEP) if not rim <= i < DEEP - rim]


def ahead_kernel(cond_in, flag, starts, tissue, fibers, pacing, wx, wy, wz, f1, f2, f3, f4, cond, sems):
    fetch([(cond_in, cond)], sems)
    before = None
    for i in range(DEEP):
        share = tissue[i].astype(jnp.float32)
        sig0 = sigma(cond, fibers[i], 0)
        wx[i] = cross_weight(sigma(cond, fibers[i], 1), share, 0)
        wy[i] = cross_weight(sigma(cond, fibers[i], 2), share, 1)
        if i:
            wz[i - 1] = face_weight(*before, sig0, share)
        before = (sig0, share)
    old = starts
    for step, new in enumerate((f1, f2, f3, f4)):
        below = None
        for i in inner_layers(step):
            v, *g = [old[n, i] for n in range(4)]
            for n, gate in enumerate(gates_next(v, *g)):
                new[n + 1, i] = gate
            if step == 0:
                low, high = i > 0, i < DEEP - 1
            else:
                low = high = step + 1 <= i < DEEP - step - 1
            if not (low or high):
                continue
            total = v + cross(v, wx[i], wy[i]) + reaction(v, *g)
            total = total + (0.6 * flag[0]) * pacing[i].astype(jnp.float32)
            if low:
                total = total - (wz[i - 1] * (v - old[0, i - 1]) if below is None else below)
            below = None
            if high:
                below = wz[i] * (old[0, i + 1] - v)
                total = total + below
            new[0, i] = total
        old = new


def forward_kernel(
    cond_in, flag, starts, tissue, fibers, pacing, wx, wy, wz, p1, p2, p3, p4, low, high,
    f1, f2, f3, f4, side, cond, sems,
):
    fetch([(cond_in, cond)], sems)
    halo = []
    for n, (msg, own) in enumerate(((low, 0), (high, DEEP - 1))):
        fib, tis = msg[FIB], msg[TIS]
        w01 = face_weight(sigma(cond, fib, 0), tis, sigma(cond, fibers[own], 0), tissue[own].astype(jnp.float32))
        side[n, C_W01] = w01
        side[n, C_WIN] = msg[WIN]
        side[n, C_WX] = cross_weight(sigma(cond, fib, 1), tis, 0)
        side[n, C_WY] = cross_weight(sigma(cond, fib, 2), tis, 1)
        halo.append(msg[V0])
        inflow = w01 * (msg[V0] - starts[0, own])
        f1[0, own] = p1[0, own] + inflow
        halo[n] = msg[P1] - inflow
        side[n, C_D1] = halo[n]
    fields = forward_fields(starts, (p1, p2, p3), (f1, f2, f3))
    for n in range(1, 4):
        for i in inner_layers(3):
            f4[n, i] = p4[n, i]
    for step in (1, 2, 3):
        old = fields[step]
        new = (f1, f2, f3, f4)[step]
        outflow = [None, None]
        above = None
        for i in rim_layers(step + 1):
            v, *g = old.all(i)
            if i not in inner_layers(step):
                for n, gate in enumerate(gates_next(v, *g)):
                    new[n + 1, i] = gate
            if i == 0:
                below = outflow[0] = side[0, C_W01] * (v - halo[0])
            elif above is not None:
                below = above
            else:
                below = wz[i - 1] * (v - old.plane(0, i - 1))
            if i == DEEP - 1:
                above = side[1, C_W01] * (halo[1] - v)
                outflow[1] = -above
            else:
                above = wz[i] * (old.plane(0, i + 1) - v)
            total = v + (above - below) + cross(v, wx[i], wy[i]) + reaction(v, *g)
            new[0, i] = total + (0.6 * flag[0]) * pacing[i].astype(jnp.float32)
            if i == step and step < 3:
                above = None
        if step == 3:
            continue
        for n, msg in enumerate((low, high)):
            v = halo[n]
            win = side[n, C_WIN]
            g = [msg[G1], msg[G2], msg[G3]]
            if step == 1:
                extra = msg[Q2]
            else:
                v1 = side[n, C_D1]
                g1 = g
                g = gates_next(v1, *g1)
                extra = msg[Q3] + win * win * v1
                t1, t2, t3 = tanhs(v1)
                side[n, C_D2] = -0.3 * (g[0] * g[1]) - 0.15 * g[2]
                side[n, C_D1] = -0.3 * (g1[0] * g1[1]) - 0.15 * g1[2]
                side[n, C_E] = (
                    0.6 * (1.0 - t1 * t1) * (0.3 * g[1] * (1.0 - v))
                    - 0.2 * (1.0 - t2 * t2) * (0.3 * g[0] * (1.0 - v))
                    - 0.06 * (1.0 - t3 * t3) * (0.15 * v)
                )
            total = v + cross(v, side[n, C_WX], side[n, C_WY]) + reaction(v, *g)
            halo[n] = total + (extra - win * v) + outflow[n]


def pull_gates(a, f):
    av, a1, a2, a3 = a
    v, g1, g2, g3 = f
    rest = 0.3 * (1.0 - v) * av
    return 0.7 * a1 + g2 * rest, 0.9 * a2 + g1 * rest, 0.97 * a3 - 0.15 * v * av


def pull_voltage(a, f):
    av, a1, a2, a3 = a
    v, g1, g2, g3 = f
    t1, t2, t3 = tanhs(v)
    total = av * (1.0 - 0.3 * (g1 * g2) - 0.15 * g3)
    total = total + 0.6 * (1.0 - t1 * t1) * a1 - 0.2 * (1.0 - t2 * t2) * a2
    return total + 0.06 * (1.0 - t3 * t3) * a3


def send_kernel(ends, following, starts, p1, p2, p3, f1, f2, f3, wx, wy, wz, gap, up, down):
    fields = forward_fields(starts, (p1, p2, p3), (f1, f2, f3))
    for n in range(4):
        for i in range(DEEP):
            gap[n, i] = ends[n, i] - following[0, n, i]
    for out, (b1, sign) in ((up, (7, -1)), (down, (0, 1))):
        layers = [b1 + sign * d for d in range(4)]
        a = [[gap[n, b] for n in range(4)] for b in layers]
        out[0] = a[0][0]
        for m in range(3):
            fresh = []
            outer = None
            for d in range(3 - m):
                b = layers[d]
                f = fields[3 - m].all(b)
                face = wz[b - 1] if sign < 0 else wz[b]
                inner = face * (a[d + 1][0] - a[d][0])
                total = pull_voltage(a[d], f) + cross(a[d][0], wx[b], wy[b]) + inner
                if outer is not None:
                    total = total - outer
                fresh.append([total, *pull_gates(a[d], f)])
                outer = inner
            a = fresh
            out[m + 1] = a[0][0]


def back_kernel(gap, starts, p1, p2, p3, f1, f2, f3, wx, wy, wz, gate, a1, a2, a3, a4):
    fields = forward_fields(starts, (p1, p2, p3), (f1, f2, f3))
    old = gap
    for m, new in enumerate((a1, a2, a3, a4)):
        below = None
        for i in inner_layers(m):
            a = [old[n, i] for n in range(4)]
            f = fields[3 - m].all(i)
            for n, plane in enumerate(pull_gates(a, f)):
                new[n + 1, i] = plane
            if i not in inner_layers(m + 1):
                continue
            if below is None:
                below = wz[i - 1] * (a[0] - old[0, i - 1])
            above = wz[i] * (old[0, i + 1] - a[0])
            new[0, i] = pull_voltage(a, f) + (above - below) + cross(a[0], wx[i], wy[i])
            below = above
        old = new


def pull_kernel(
    starts, gap, before, p1, p2, p3, f1, f2, f3, b1, b2, b3, b4, wx, wy, wz, side, low, high,
    defect_out, gradient_out, work, defect, gradient, sems,
):
    for n in range(4):
        for i in range(DEEP):
            defect[n, i] = before[0, n, i] - starts[n, i]
    copies = [pltpu.make_async_copy(defect, defect_out.at[0], sems.at[DEEP])]
    copies[0].start()
    fields = forward_fields(starts, (p1, p2, p3), (f1, f2, f3))
    adjoints = [Fields(gap, None, 0, 0)] + [
        Fields(b, work.at[j], j + 1, j) for j, b in enumerate((b1, b2, b3))
    ]
    halo = [low[0], high[0]]
    first = [None, None]
    last = [None, None]
    for m in range(4):
        old = adjoints[m]
        outflow = [None, None]
        above = None
        for i in rim_layers(m + 1):
            a = old.all(i)
            f = fields[3 - m].all(i)
            if i == 0:
                below = outflow[0] = side[0, C_W01] * (a[0] - halo[0])
            elif above is not None:
                below = above
            else:
                below = wz[i - 1] * (a[0] - old.plane(0, i - 1))
            if i == DEEP - 1:
                above = side[1, C_W01] * (halo[1] - a[0])
                outflow[1] = -above
            else:
                above = wz[i] * (old.plane(0, i + 1) - a[0])
            fresh = [pull_voltage(a, f) + (above - below) + cross(a[0], wx[i], wy[i])]
            if i in inner_layers(m):
                if m == 3:
                    fresh += [b4[n, i] for n in (1, 2, 3)]
            else:
                fresh += pull_gates(a, f)
            if i == m and m < 3:
                above = None
            if m < 3:
                for n, plane in enumerate(fresh):
                    work[m, n, i] = plane
                continue
            for n, plane in enumerate(fresh):
                gradient[n, i] = plane - defect[n, i]
            copy = pltpu.make_async_copy(gradient.at[:, i], gradient_out.at[0, :, i], sems.at[i])
            copy.start()
            copies.append(copy)
        if m == 3:
            continue
        for n, msg in enumerate((low, high)):
            win, px, py = side[n, C_WIN], side[n, C_WX], side[n, C_WY]
            if m == 0:
                change = first[n] = outflow[n]
            else:
                d = last[n]
                rate = side[n, C_D2] if m == 1 else side[n, C_D1]
                change = d + cross(d, px, py) + (rate - win) * d + outflow[n]
                if m == 2:
                    change = change + (win * win + side[n, C_E]) * first[n]
            halo[n] = msg[m + 1] + change
            last[n] = change
    for copy in copies:
        copy.wait()


VM = pl.BlockSpec(memory_space=pltpu.VMEM)
SM = pl.BlockSpec(memory_space=pltpu.SMEM)
ANY = pl.BlockSpec(memory_space=pl.ANY)


def f32(*shape):
    return jax.ShapeDtypeStruct(shape, jnp.float32)


def i32(*shape):
    return jax.ShapeDtypeStruct(shape, jnp.int32)


def call(kernel, name, ins, outs, scratch=(), out_spec=VM):
    return pl.pallas_call(
        kernel,
        name=name,
        in_specs=ins,
        out_specs=[out_spec] * len(outs),
        out_shape=outs,
        scratch_shapes=list(scratch),
        compiler_params=pltpu.CompilerParams(vmem_limit_bytes=28 * 1024 * 1024),
    )


def body(starts, tissue, fibers, pacing, conductances):
    plane = (NX, NY)
    slab = (DEEP, *plane)
    fields = f32(4, *slab)
    slabs = lax.axis_size("slab")
    sections = lax.axis_size("tm")
    upward = [(i, i + 1) for i in range(slabs - 1)]
    downward = [(i + 1, i) for i in range(slabs - 1)]
    earlier = [((i + 1) % sections, i) for i in range(sections)]
    later = [(i, (i + 1) % sections) for i in range(sections)]
    flag = (lax.axis_index("tm") == 0).astype(jnp.float32).reshape(1)
    few = [pltpu.SMEM((4, 3), jnp.float32), pltpu.SemaphoreType.DMA((1,))]

    up, down, own, tis, fib, pac = call(
        edge_kernel,
        "edge",
        [ANY, SM] + [ANY] * 4,
        [f32(10, *plane)] * 2 + [fields] + [i32(*slab)] * 3,
        [pltpu.SMEM((4, 3), jnp.float32), pltpu.SemaphoreType.DMA((5,))],
    )(conductances, flag, starts, tissue, fibers, pacing)
    low = lax.ppermute(up, "slab", upward)
    high = lax.ppermute(down, "slab", downward)
    following = lax.ppermute(starts, "tm", earlier)
    wx, wy, wz, p1, p2, p3, p4 = call(
        ahead_kernel,
        "ahead",
        [ANY, SM] + [VM] * 4,
        [f32(*slab), f32(*slab), f32(DEEP - 1, *plane)] + [fields] * 4,
        few,
    )(conductances, flag, own, tis, fib, pac)
    f1, f2, f3, ends, side = call(
        forward_kernel,
        "forward",
        [ANY, SM] + [VM] * 13,
        [fields] * 4 + [f32(2, 7, *plane)],
        few,
    )(conductances, flag, own, tis, fib, pac, wx, wy, wz, p1, p2, p3, p4, low, high)
    before = lax.ppermute(ends[None], "tm", later)
    history = (own, p1, p2, p3, f1, f2, f3)
    gap, up, down = call(
        send_kernel, "send", [VM] * 12, [fields, f32(4, *plane), f32(4, *plane)]
    )(ends, following, *history, wx, wy, wz)
    low = lax.ppermute(up, "slab", upward)
    high = lax.ppermute(down, "slab", downward)
    inner = call(back_kernel, "back", [VM] * 11 + [ANY], [fields] * 4)(gap, *history, wx, wy, wz, up)
    defect, gradient = call(
        pull_kernel,
        "pull",
        [VM] * 19,
        [f32(1, 4, *slab)] * 2,
        [pltpu.VMEM((3, 4, *slab), jnp.float32)]
        + [pltpu.VMEM((4, *slab), jnp.float32)] * 2
        + [pltpu.SemaphoreType.DMA((DEEP + 1,))],
        ANY,
    )(own, gap, before, p1, p2, p3, f1, f2, f3, *inner, wx, wy, wz, side, low, high)
    return defect, gradient


def solution(mesh):
    spread = P("tm", None, "slab", None, None)
    placed = (spread, P("slab", None, None), P("slab", None, None), P("slab", None, None), P())
    return jax.shard_map(body, mesh=mesh, in_specs=placed, out_specs=(spread, spread), check_vma=False)
```

```python
import jax
import jax.numpy as jnp
from jax import lax
from jax.experimental import pallas as pl
from jax.experimental.pallas import tpu as pltpu
from jax.sharding import PartitionSpec as P

DEEP = 8
NX = 64
NY = 128
V0, P1, G1, G2, G3, Q2, Q3, FIB, TIS, WIN = range(10)
C_W01, C_WIN, C_WX, C_WY, C_D2, C_E, C_D1 = range(7)
HALF_STEP = 0.15 * 0.5


def ahead(plane, axis):
    return pltpu.roll(plane, plane.shape[axis] - 1, axis)


def behind(plane, axis):
    return pltpu.roll(plane, 1, axis)


def sigma(cond, fiber, direction):
    summed = jnp.zeros(fiber.shape, jnp.float32)
    for c in range(4):
        summed = jnp.where(fiber == c, cond[c, direction], summed)
    return summed


def cross_weight(sig, share, axis):
    place = lax.broadcasted_iota(jnp.int32, sig.shape, axis)
    inner = jnp.where(place < sig.shape[axis] - 1, HALF_STEP, 0.0)
    return inner * (sig + ahead(sig, axis)) * (share * ahead(share, axis))


def face_weight(sig_a, share_a, sig_b, share_b):
    return HALF_STEP * (sig_a + sig_b) * (share_a * share_b)


def cross(v, wx, wy):
    fx = wx * (ahead(v, 0) - v)
    fy = wy * (ahead(v, 1) - v)
    return (fx - behind(fx, 0)) + (fy - behind(fy, 1))


def reaction(v, g1, g2, g3):
    return 0.3 * (g1 * g2) * (1.0 - v) - 0.15 * g3 * v


def tanhs(v):
    return jnp.tanh(4.0 * v - 0.8), jnp.tanh(2.0 - 4.0 * v), jnp.tanh(4.0 * v - 3.2)


def gates_next(v, g1, g2, g3):
    t1, t2, t3 = tanhs(v)
    return (
        0.7 * g1 + (0.15 + 0.15 * t1),
        0.9 * g2 + (0.05 + 0.05 * t2),
        0.97 * g3 + (0.015 + 0.015 * t3),
    )


def fetch(copies, sems):
    started = [pltpu.make_async_copy(src, dst, sems.at[n]) for n, (src, dst) in enumerate(copies)]
    for copy in started:
        copy.start()
    for copy in started:
        copy.wait()


def edge_kernel(
    cond_in, flag, starts_in, tissue_in, fibers_in, pacing_in, up, down, starts, tissue, fibers, pacing, cond, sems
):
    fetch(
        [
            (starts_in.at[0], starts),
            (tissue_in, tissue),
            (fibers_in, fibers),
            (pacing_in, pacing),
            (cond_in, cond),
        ],
        sems,
    )
    for out, (b1, b2, b3, b4) in ((up, (7, 6, 5, 4)), (down, (0, 1, 2, 3))):
        share = [tissue[b].astype(jnp.float32) for b in (b1, b2, b3, b4)]
        sig0 = [sigma(cond, fibers[b], 0) for b in (b1, b2, b3, b4)]
        wz = [face_weight(sig0[i], share[i], sig0[i + 1], share[i + 1]) for i in range(3)]
        wx = [cross_weight(sigma(cond, fibers[b], 1), share[i], 0) for i, b in enumerate((b1, b2, b3))]
        wy = [cross_weight(sigma(cond, fibers[b], 2), share[i], 1) for i, b in enumerate((b1, b2, b3))]
        stim = [(0.6 * flag[0]) * pacing[b].astype(jnp.float32) for b in (b1, b2, b3)]
        v = [starts[0, b] for b in (b1, b2, b3, b4)]
        g = [[starts[n, b] for n in (1, 2, 3)] for b in (b1, b2, b3)]

        def own_step(i):
            total = v[i] + cross(v[i], wx[i], wy[i]) + reaction(v[i], *g[i]) + stim[i]
            total = total + wz[i] * (v[i + 1] - v[i])
            return total if i == 0 else total + wz[i - 1] * (v[i - 1] - v[i])

        out[V0] = v[0]
        out[P1] = own_step(0)
        gates = gates_next(v[0], *g[0])
        for n in range(3):
            out[G1 + n] = gates[n]
        v1_b2 = own_step(1)
        v1_b3 = own_step(2)
        out[Q2] = wz[0] * v1_b2 + stim[0]
        rest = v1_b2 + cross(v1_b2, wx[1], wy[1]) + reaction(v1_b2, *gates_next(v[1], *g[1])) + stim[1]
        rest = rest + wz[1] * (v1_b3 - v1_b2) - wz[0] * v1_b2
        out[Q3] = wz[0] * rest + stim[0]
        out[FIB] = fibers[b1].astype(jnp.float32)
        out[TIS] = share[0]
        out[WIN] = wz[0]


class Fields:
    def __init__(self, inner, outer, rim_voltage, rim_gate):
        self.refs = (inner, outer)
        self.rims = (rim_voltage, rim_gate)

    def plane(self, field, layer):
        rim = self.rims[0] if field == 0 else self.rims[1]
        inside = rim <= layer < DEEP - rim
        return self.refs[0 if inside else 1][field, layer]

    def all(self, layer):
        return [self.plane(n, layer) for n in range(4)]


def forward_fields(starts, inner, outer):
    return [Fields(starts, None, 0, 0)] + [Fields(inner[j - 1], outer[j - 1], j, j - 1) for j in (1, 2, 3)]


def inner_layers(rim):
    return range(rim, DEEP - rim)


def rim_layers(rim):
    return [i for i in range(DEEP) if not rim <= i < DEEP - rim]


def ahead_kernel(cond_in, flag, starts, tissue, fibers, pacing, wx, wy, wz, f1, f2, f3, f4, cond, sems):
    fetch([(cond_in, cond)], sems)
    before = None
    for i in range(DEEP):
        share = tissue[i].astype(jnp.float32)
        sig0 = sigma(cond, fibers[i], 0)
        wx[i] = cross_weight(sigma(cond, fibers[i], 1), share, 0)
        wy[i] = cross_weight(sigma(cond, fibers[i], 2), share, 1)
        if i:
            wz[i - 1] = face_weight(*before, sig0, share)
        before = (sig0, share)
    old = starts
    for step, new in enumerate((f1, f2, f3, f4)):
        below = None
        for i in inner_layers(step):
            v, *g = [old[n, i] for n in range(4)]
            for n, gate in enumerate(gates_next(v, *g)):
                new[n + 1, i] = gate
            if step == 0:
                low, high = i > 0, i < DEEP - 1
            else:
                low = high = step + 1 <= i < DEEP - step - 1
            if not (low or high):
                continue
            total = v + cross(v, wx[i], wy[i]) + reaction(v, *g)
            total = total + (0.6 * flag[0]) * pacing[i].astype(jnp.float32)
            if low:
                total = total - (wz[i - 1] * (v - old[0, i - 1]) if below is None else below)
            below = None
            if high:
                below = wz[i] * (old[0, i + 1] - v)
                total = total + below
            new[0, i] = total
        old = new


def forward_kernel(
    cond_in, flag, starts, tissue, fibers, pacing, wx, wy, wz, p1, p2, p3, p4, low, high,
    f1, f2, f3, f4, side, cond, sems,
):
    fetch([(cond_in, cond)], sems)
    halo = []
    for n, (msg, own) in enumerate(((low, 0), (high, DEEP - 1))):
        fib, tis = msg[FIB], msg[TIS]
        w01 = face_weight(sigma(cond, fib, 0), tis, sigma(cond, fibers[own], 0), tissue[own].astype(jnp.float32))
        side[n, C_W01] = w01
        side[n, C_WIN] = msg[WIN]
        side[n, C_WX] = cross_weight(sigma(cond, fib, 1), tis, 0)
        side[n, C_WY] = cross_weight(sigma(cond, fib, 2), tis, 1)
        halo.append(msg[V0])
        inflow = w01 * (msg[V0] - starts[0, own])
        f1[0, own] = p1[0, own] + inflow
        halo[n] = msg[P1] - inflow
        side[n, C_D1] = halo[n]
    fields = forward_fields(starts, (p1, p2, p3), (f1, f2, f3))
    for n in range(1, 4):
        for i in inner_layers(3):
            f4[n, i] = p4[n, i]
    for step in (1, 2, 3):
        old = fields[step]
        new = (f1, f2, f3, f4)[step]
        outflow = [None, None]
        above = None
        for i in rim_layers(step + 1):
            v, *g = old.all(i)
            if i not in inner_layers(step):
                for n, gate in enumerate(gates_next(v, *g)):
                    new[n + 1, i] = gate
            if i == 0:
                below = outflow[0] = side[0, C_W01] * (v - halo[0])
            elif above is not None:
                below = above
            else:
                below = wz[i - 1] * (v - old.plane(0, i - 1))
            if i == DEEP - 1:
                above = side[1, C_W01] * (halo[1] - v)
                outflow[1] = -above
            else:
                above = wz[i] * (old.plane(0, i + 1) - v)
            total = v + (above - below) + cross(v, wx[i], wy[i]) + reaction(v, *g)
            new[0, i] = total + (0.6 * flag[0]) * pacing[i].astype(jnp.float32)
            if i == step and step < 3:
                above = None
        if step == 3:
            continue
        for n, msg in enumerate((low, high)):
            v = halo[n]
            win = side[n, C_WIN]
            g = [msg[G1], msg[G2], msg[G3]]
            if step == 1:
                extra = msg[Q2]
            else:
                v1 = side[n, C_D1]
                g1 = g
                g = gates_next(v1, *g1)
                extra = msg[Q3] + win * win * v1
                t1, t2, t3 = tanhs(v1)
                side[n, C_D2] = -0.3 * (g[0] * g[1]) - 0.15 * g[2]
                side[n, C_D1] = -0.3 * (g1[0] * g1[1]) - 0.15 * g1[2]
                side[n, C_E] = (
                    0.6 * (1.0 - t1 * t1) * (0.3 * g[1] * (1.0 - v))
                    - 0.2 * (1.0 - t2 * t2) * (0.3 * g[0] * (1.0 - v))
                    - 0.06 * (1.0 - t3 * t3) * (0.15 * v)
                )
            total = v + cross(v, side[n, C_WX], side[n, C_WY]) + reaction(v, *g)
            halo[n] = total + (extra - win * v) + outflow[n]


def pull_gates(a, f):
    av, a1, a2, a3 = a
    v, g1, g2, g3 = f
    rest = 0.3 * (1.0 - v) * av
    return 0.7 * a1 + g2 * rest, 0.9 * a2 + g1 * rest, 0.97 * a3 - 0.15 * v * av


def pull_voltage(a, f):
    av, a1, a2, a3 = a
    v, g1, g2, g3 = f
    t1, t2, t3 = tanhs(v)
    total = av * (1.0 - 0.3 * (g1 * g2) - 0.15 * g3)
    total = total + 0.6 * (1.0 - t1 * t1) * a1 - 0.2 * (1.0 - t2 * t2) * a2
    return total + 0.06 * (1.0 - t3 * t3) * a3


def send_kernel(ends, following, starts, p1, p2, p3, f1, f2, f3, wx, wy, wz, gap, up, down):
    fields = forward_fields(starts, (p1, p2, p3), (f1, f2, f3))
    for n in range(4):
        for i in range(DEEP):
            gap[n, i] = ends[n, i] - following[0, n, i]
    for out, (b1, sign) in ((up, (7, -1)), (down, (0, 1))):
        layers = [b1 + sign * d for d in range(4)]
        a = [[gap[n, b] for n in range(4)] for b in layers]
        out[0] = a[0][0]
        for m in range(3):
            fresh = []
            outer = None
            for d in range(3 - m):
                b = layers[d]
                f = fields[3 - m].all(b)
                face = wz[b - 1] if sign < 0 else wz[b]
                inner = face * (a[d + 1][0] - a[d][0])
                total = pull_voltage(a[d], f) + cross(a[d][0], wx[b], wy[b]) + inner
                if outer is not None:
                    total = total - outer
                fresh.append([total, *pull_gates(a[d], f)])
                outer = inner
            a = fresh
            out[m + 1] = a[0][0]


def back_kernel(gap, starts, p1, p2, p3, f1, f2, f3, wx, wy, wz, gate, a1, a2, a3, a4):
    fields = forward_fields(starts, (p1, p2, p3), (f1, f2, f3))
    old = gap
    for m, new in enumerate((a1, a2, a3, a4)):
        below = None
        for i in inner_layers(m):
            a = [old[n, i] for n in range(4)]
            f = fields[3 - m].all(i)
            for n, plane in enumerate(pull_gates(a, f)):
                new[n + 1, i] = plane
            if i not in inner_layers(m + 1):
                continue
            if below is None:
                below = wz[i - 1] * (a[0] - old[0, i - 1])
            above = wz[i] * (old[0, i + 1] - a[0])
            new[0, i] = pull_voltage(a, f) + (above - below) + cross(a[0], wx[i], wy[i])
            below = above
        old = new


def pull_kernel(
    starts, gap, before, p1, p2, p3, f1, f2, f3, b1, b2, b3, b4, wx, wy, wz, side, low, high,
    defect_out, gradient_out, work, defect, gradient, sems,
):
    for n in range(4):
        for i in range(DEEP):
            defect[n, i] = before[0, n, i] - starts[n, i]
    copies = [pltpu.make_async_copy(defect, defect_out.at[0], sems.at[DEEP])]
    copies[0].start()
    fields = forward_fields(starts, (p1, p2, p3), (f1, f2, f3))
    adjoints = [Fields(gap, None, 0, 0)] + [
        Fields(b, work.at[j], j + 1, j) for j, b in enumerate((b1, b2, b3))
    ]
    halo = [low[0], high[0]]
    first = [None, None]
    last = [None, None]
    for m in range(4):
        old = adjoints[m]
        outflow = [None, None]
        above = None
        for i in rim_layers(m + 1):
            a = old.all(i)
            f = fields[3 - m].all(i)
            if i == 0:
                below = outflow[0] = side[0, C_W01] * (a[0] - halo[0])
            elif above is not None:
                below = above
            else:
                below = wz[i - 1] * (a[0] - old.plane(0, i - 1))
            if i == DEEP - 1:
                above = side[1, C_W01] * (halo[1] - a[0])
                outflow[1] = -above
            else:
                above = wz[i] * (old.plane(0, i + 1) - a[0])
            fresh = [pull_voltage(a, f) + (above - below) + cross(a[0], wx[i], wy[i])]
            if i in inner_layers(m):
                if m == 3:
                    fresh += [b4[n, i] for n in (1, 2, 3)]
            else:
                fresh += pull_gates(a, f)
            if i == m and m < 3:
                above = None
            if m < 3:
                for n, plane in enumerate(fresh):
                    work[m, n, i] = plane
                continue
            for n, plane in enumerate(fresh):
                gradient[n, i] = plane - defect[n, i]
            copy = pltpu.make_async_copy(gradient.at[:, i], gradient_out.at[0, :, i], sems.at[i])
            copy.start()
            copies.append(copy)
        if m == 3:
            continue
        for n, msg in enumerate((low, high)):
            win, px, py = side[n, C_WIN], side[n, C_WX], side[n, C_WY]
            if m == 0:
                change = first[n] = outflow[n]
            else:
                d = last[n]
                rate = side[n, C_D2] if m == 1 else side[n, C_D1]
                change = d + cross(d, px, py) + (rate - win) * d + outflow[n]
                if m == 2:
                    change = change + (win * win + side[n, C_E]) * first[n]
            halo[n] = msg[m + 1] + change
            last[n] = change
    for copy in copies:
        copy.wait()


VM = pl.BlockSpec(memory_space=pltpu.VMEM)
SM = pl.BlockSpec(memory_space=pltpu.SMEM)
ANY = pl.BlockSpec(memory_space=pl.ANY)
HBM = pl.BlockSpec(memory_space=pltpu.HBM)


def f32(*shape):
    return jax.ShapeDtypeStruct(shape, jnp.float32)


def i32(*shape):
    return jax.ShapeDtypeStruct(shape, jnp.int32)


def call(kernel, name, ins, outs, scratch=(), out_spec=VM):
    return pl.pallas_call(
        kernel,
        name=name,
        in_specs=ins,
        out_specs=[out_spec] * len(outs),
        out_shape=outs,
        scratch_shapes=list(scratch),
        compiler_params=pltpu.CompilerParams(vmem_limit_bytes=28 * 1024 * 1024),
    )


def body(starts, tissue, fibers, pacing, conductances):
    plane = (NX, NY)
    slab = (DEEP, *plane)
    fields = f32(4, *slab)
    slabs = lax.axis_size("slab")
    sections = lax.axis_size("tm")
    upward = [(i, i + 1) for i in range(slabs - 1)]
    downward = [(i + 1, i) for i in range(slabs - 1)]
    earlier = [((i + 1) % sections, i) for i in range(sections)]
    later = [(i, (i + 1) % sections) for i in range(sections)]
    flag = (lax.axis_index("tm") == 0).astype(jnp.float32).reshape(1)
    few = [pltpu.SMEM((4, 3), jnp.float32), pltpu.SemaphoreType.DMA((1,))]

    conductances, starts, tissue, fibers, pacing = (
        pltpu.with_memory_space_constraint(arg, pltpu.HBM)
        for arg in (conductances, starts, tissue, fibers, pacing)
    )
    up, down, own, tis, fib, pac = call(
        edge_kernel,
        "edge",
        [HBM, SM] + [HBM] * 4,
        [f32(10, *plane)] * 2 + [fields] + [i32(*slab)] * 3,
        [pltpu.SMEM((4, 3), jnp.float32), pltpu.SemaphoreType.DMA((5,))],
    )(conductances, flag, starts, tissue, fibers, pacing)
    low = lax.ppermute(up, "slab", upward)
    high = lax.ppermute(down, "slab", downward)
    following = lax.ppermute(own[None], "tm", earlier)
    wx, wy, wz, p1, p2, p3, p4 = call(
        ahead_kernel,
        "ahead",
        [HBM, SM] + [VM] * 4,
        [f32(*slab), f32(*slab), f32(DEEP - 1, *plane)] + [fields] * 4,
        few,
    )(conductances, flag, own, tis, fib, pac)
    f1, f2, f3, ends, side = call(
        forward_kernel,
        "forward",
        [HBM, SM] + [VM] * 13,
        [fields] * 4 + [f32(2, 7, *plane)],
        few,
    )(conductances, flag, own, tis, fib, pac, wx, wy, wz, p1, p2, p3, p4, low, high)
    before = lax.ppermute(ends[None], "tm", later)
    history = (own, p1, p2, p3, f1, f2, f3)
    gap, up, down = call(
        send_kernel, "send", [VM] * 12, [fields, f32(4, *plane), f32(4, *plane)]
    )(ends, following, *history, wx, wy, wz)
    low = lax.ppermute(up, "slab", upward)
    high = lax.ppermute(down, "slab", downward)
    inner = call(back_kernel, "back", [VM] * 11 + [ANY], [fields] * 4)(gap, *history, wx, wy, wz, up)
    defect, gradient = call(
        pull_kernel,
        "pull",
        [VM] * 19,
        [f32(1, 4, *slab)] * 2,
        [pltpu.VMEM((3, 4, *slab), jnp.float32)]
        + [pltpu.VMEM((4, *slab), jnp.float32)] * 2
        + [pltpu.SemaphoreType.DMA((DEEP + 1,))],
        ANY,
    )(own, gap, before, p1, p2, p3, f1, f2, f3, *inner, wx, wy, wz, side, low, high)
    return defect, gradient


def solution(mesh):
    spread = P("tm", None, "slab", None, None)
    placed = (spread, P("slab", None, None), P("slab", None, None), P("slab", None, None), P())
    return jax.shard_map(body, mesh=mesh, in_specs=placed, out_specs=(spread, spread), check_vma=False)
```

```python
import jax
import jax.numpy as jnp
from jax import lax
from jax.experimental import pallas as pl
from jax.experimental.pallas import tpu as pltpu
from jax.sharding import PartitionSpec as P

DEEP = 8
NX = 64
NY = 128
V0, P1, G1, G2, G3, Q2, Q3 = range(7)
FIB, TIS, WIN = range(3)
C_W01, C_WIN, C_WX, C_WY, C_D2, C_E, C_D1 = range(7)
HALF_STEP = 0.15 * 0.5


def ahead(plane, axis):
    return pltpu.roll(plane, plane.shape[axis] - 1, axis)


def behind(plane, axis):
    return pltpu.roll(plane, 1, axis)


def sigma(cond, fiber, direction):
    summed = jnp.zeros(fiber.shape, jnp.float32)
    for c in range(4):
        summed = jnp.where(fiber == c, cond[c, direction], summed)
    return summed


def cross_weight(sig, share, axis):
    place = lax.broadcasted_iota(jnp.int32, sig.shape, axis)
    inner = jnp.where(place < sig.shape[axis] - 1, HALF_STEP, 0.0)
    return inner * (sig + ahead(sig, axis)) * (share * ahead(share, axis))


def face_weight(sig_a, share_a, sig_b, share_b):
    return HALF_STEP * (sig_a + sig_b) * (share_a * share_b)


def cross(v, wx, wy):
    fx = wx * (ahead(v, 0) - v)
    fy = wy * (ahead(v, 1) - v)
    return (fx - behind(fx, 0)) + (fy - behind(fy, 1))


def reaction(v, g1, g2, g3):
    return 0.3 * (g1 * g2) * (1.0 - v) - 0.15 * g3 * v


def tanhs(v):
    return jnp.tanh(4.0 * v - 0.8), jnp.tanh(2.0 - 4.0 * v), jnp.tanh(4.0 * v - 3.2)


def gates_next(v, g1, g2, g3):
    t1, t2, t3 = tanhs(v)
    return (
        0.7 * g1 + (0.15 + 0.15 * t1),
        0.9 * g2 + (0.05 + 0.05 * t2),
        0.97 * g3 + (0.015 + 0.015 * t3),
    )


def fetch(copies, sems):
    started = [pltpu.make_async_copy(src, dst, sems.at[n]) for n, (src, dst) in enumerate(copies)]
    for copy in started:
        copy.start()
    for copy in started:
        copy.wait()


def edge_kernel(
    cond_in, flag, starts_in, tissue_in, fibers_in, pacing_in,
    up, down, up_tissue, down_tissue, starts, tissue, fibers, pacing, cond, sems,
):
    fetch(
        [
            (starts_in.at[0], starts),
            (tissue_in, tissue),
            (fibers_in, fibers),
            (pacing_in, pacing),
            (cond_in, cond),
        ],
        sems,
    )
    for out, out_tissue, (b1, b2, b3, b4) in (
        (up, up_tissue, (7, 6, 5, 4)),
        (down, down_tissue, (0, 1, 2, 3)),
    ):
        share = [tissue[b].astype(jnp.float32) for b in (b1, b2, b3, b4)]
        sig0 = [sigma(cond, fibers[b], 0) for b in (b1, b2, b3, b4)]
        wz = [face_weight(sig0[i], share[i], sig0[i + 1], share[i + 1]) for i in range(3)]
        wx = [cross_weight(sigma(cond, fibers[b], 1), share[i], 0) for i, b in enumerate((b1, b2, b3))]
        wy = [cross_weight(sigma(cond, fibers[b], 2), share[i], 1) for i, b in enumerate((b1, b2, b3))]
        stim = [(0.6 * flag[0]) * pacing[b].astype(jnp.float32) for b in (b1, b2, b3)]
        v = [starts[0, b] for b in (b1, b2, b3, b4)]
        g = [[starts[n, b] for n in (1, 2, 3)] for b in (b1, b2, b3)]

        def own_step(i):
            total = v[i] + cross(v[i], wx[i], wy[i]) + reaction(v[i], *g[i]) + stim[i]
            total = total + wz[i] * (v[i + 1] - v[i])
            return total if i == 0 else total + wz[i - 1] * (v[i - 1] - v[i])

        out[V0] = v[0]
        out[P1] = own_step(0)
        gates = gates_next(v[0], *g[0])
        for n in range(3):
            out[G1 + n] = gates[n]
        v1_b2 = own_step(1)
        v1_b3 = own_step(2)
        out[Q2] = wz[0] * v1_b2 + stim[0]
        rest = v1_b2 + cross(v1_b2, wx[1], wy[1]) + reaction(v1_b2, *gates_next(v[1], *g[1])) + stim[1]
        rest = rest + wz[1] * (v1_b3 - v1_b2) - wz[0] * v1_b2
        out[Q3] = wz[0] * rest + stim[0]
        out_tissue[FIB] = fibers[b1].astype(jnp.float32)
        out_tissue[TIS] = share[0]
        out_tissue[WIN] = wz[0]


class Fields:
    def __init__(self, inner, outer, rim_voltage, rim_gate):
        self.refs = (inner, outer)
        self.rims = (rim_voltage, rim_gate)

    def plane(self, field, layer):
        rim = self.rims[0] if field == 0 else self.rims[1]
        inside = rim <= layer < DEEP - rim
        return self.refs[0 if inside else 1][field, layer]

    def all(self, layer):
        return [self.plane(n, layer) for n in range(4)]


def forward_fields(starts, inner, outer):
    return [Fields(starts, None, 0, 0)] + [Fields(inner[j - 1], outer[j - 1], j, j - 1) for j in (1, 2, 3)]


def inner_layers(rim):
    return range(rim, DEEP - rim)


def rim_layers(rim):
    return [i for i in range(DEEP) if not rim <= i < DEEP - rim]


def ahead_kernel(cond_in, flag, starts, tissue, fibers, pacing, wx, wy, wz, f1, f2, f3, f4, cond, sems):
    fetch([(cond_in, cond)], sems)
    before = None
    for i in range(DEEP):
        share = tissue[i].astype(jnp.float32)
        sig0 = sigma(cond, fibers[i], 0)
        wx[i] = cross_weight(sigma(cond, fibers[i], 1), share, 0)
        wy[i] = cross_weight(sigma(cond, fibers[i], 2), share, 1)
        if i:
            wz[i - 1] = face_weight(*before, sig0, share)
        before = (sig0, share)
    old = starts
    for step, new in enumerate((f1, f2, f3, f4)):
        below = None
        for i in inner_layers(step):
            v, *g = [old[n, i] for n in range(4)]
            for n, gate in enumerate(gates_next(v, *g)):
                new[n + 1, i] = gate
            if step == 0:
                low, high = i > 0, i < DEEP - 1
            else:
                low = high = step + 1 <= i < DEEP - step - 1
            if not (low or high):
                continue
            total = v + cross(v, wx[i], wy[i]) + reaction(v, *g)
            total = total + (0.6 * flag[0]) * pacing[i].astype(jnp.float32)
            if low:
                total = total - (wz[i - 1] * (v - old[0, i - 1]) if below is None else below)
            below = None
            if high:
                below = wz[i] * (old[0, i + 1] - v)
                total = total + below
            new[0, i] = total
        old = new


def forward_kernel(
    cond_in, flag, starts, tissue, fibers, pacing, wx, wy, wz, p1, p2, p3, p4, low, high, low_tissue, high_tissue,
    f1, f2, f3, f4, side, cond, sems,
):
    fetch([(cond_in, cond)], sems)
    halo = []
    for n, (msg, beside, own) in enumerate(((low, low_tissue, 0), (high, high_tissue, DEEP - 1))):
        fib, tis = beside[FIB], beside[TIS]
        w01 = face_weight(sigma(cond, fib, 0), tis, sigma(cond, fibers[own], 0), tissue[own].astype(jnp.float32))
        side[n, C_W01] = w01
        side[n, C_WIN] = beside[WIN]
        side[n, C_WX] = cross_weight(sigma(cond, fib, 1), tis, 0)
        side[n, C_WY] = cross_weight(sigma(cond, fib, 2), tis, 1)
        halo.append(msg[V0])
        inflow = w01 * (msg[V0] - starts[0, own])
        f1[0, own] = p1[0, own] + inflow
        halo[n] = msg[P1] - inflow
        side[n, C_D1] = halo[n]
    fields = forward_fields(starts, (p1, p2, p3), (f1, f2, f3))
    for n in range(1, 4):
        for i in inner_layers(3):
            f4[n, i] = p4[n, i]
    for step in (1, 2, 3):
        old = fields[step]
        new = (f1, f2, f3, f4)[step]
        outflow = [None, None]
        above = None
        for i in rim_layers(step + 1):
            v, *g = old.all(i)
            if i not in inner_layers(step):
                for n, gate in enumerate(gates_next(v, *g)):
                    new[n + 1, i] = gate
            if i == 0:
                below = outflow[0] = side[0, C_W01] * (v - halo[0])
            elif above is not None:
                below = above
            else:
                below = wz[i - 1] * (v - old.plane(0, i - 1))
            if i == DEEP - 1:
                above = side[1, C_W01] * (halo[1] - v)
                outflow[1] = -above
            else:
                above = wz[i] * (old.plane(0, i + 1) - v)
            total = v + (above - below) + cross(v, wx[i], wy[i]) + reaction(v, *g)
            new[0, i] = total + (0.6 * flag[0]) * pacing[i].astype(jnp.float32)
            if i == step and step < 3:
                above = None
        if step == 3:
            continue
        for n, msg in enumerate((low, high)):
            v = halo[n]
            win = side[n, C_WIN]
            g = [msg[G1], msg[G2], msg[G3]]
            if step == 1:
                extra = msg[Q2]
            else:
                v1 = side[n, C_D1]
                g1 = g
                g = gates_next(v1, *g1)
                extra = msg[Q3] + win * win * v1
                t1, t2, t3 = tanhs(v1)
                side[n, C_D2] = -0.3 * (g[0] * g[1]) - 0.15 * g[2]
                side[n, C_D1] = -0.3 * (g1[0] * g1[1]) - 0.15 * g1[2]
                side[n, C_E] = (
                    0.6 * (1.0 - t1 * t1) * (0.3 * g[1] * (1.0 - v))
                    - 0.2 * (1.0 - t2 * t2) * (0.3 * g[0] * (1.0 - v))
                    - 0.06 * (1.0 - t3 * t3) * (0.15 * v)
                )
            total = v + cross(v, side[n, C_WX], side[n, C_WY]) + reaction(v, *g)
            halo[n] = total + (extra - win * v) + outflow[n]


def pull_gates(a, f):
    av, a1, a2, a3 = a
    v, g1, g2, g3 = f
    rest = 0.3 * (1.0 - v) * av
    return 0.7 * a1 + g2 * rest, 0.9 * a2 + g1 * rest, 0.97 * a3 - 0.15 * v * av


def pull_voltage(a, f):
    av, a1, a2, a3 = a
    v, g1, g2, g3 = f
    t1, t2, t3 = tanhs(v)
    total = av * (1.0 - 0.3 * (g1 * g2) - 0.15 * g3)
    total = total + 0.6 * (1.0 - t1 * t1) * a1 - 0.2 * (1.0 - t2 * t2) * a2
    return total + 0.06 * (1.0 - t3 * t3) * a3


def send_kernel(ends, following, starts, p1, p2, p3, f1, f2, f3, wx, wy, wz, gap, up, down):
    fields = forward_fields(starts, (p1, p2, p3), (f1, f2, f3))
    for n in range(4):
        for i in range(DEEP):
            gap[n, i] = ends[n, i] - following[0, n, i]
    for out, (b1, sign) in ((up, (7, -1)), (down, (0, 1))):
        layers = [b1 + sign * d for d in range(4)]
        a = [[gap[n, b] for n in range(4)] for b in layers]
        out[0] = a[0][0]
        for m in range(3):
            fresh = []
            outer = None
            for d in range(3 - m):
                b = layers[d]
                f = fields[3 - m].all(b)
                face = wz[b - 1] if sign < 0 else wz[b]
                inner = face * (a[d + 1][0] - a[d][0])
                total = pull_voltage(a[d], f) + cross(a[d][0], wx[b], wy[b]) + inner
                if outer is not None:
                    total = total - outer
                fresh.append([total, *pull_gates(a[d], f)])
                outer = inner
            a = fresh
            out[m + 1] = a[0][0]


def back_kernel(gap, starts, p1, p2, p3, f1, f2, f3, wx, wy, wz, gate, a1, a2, a3, a4):
    fields = forward_fields(starts, (p1, p2, p3), (f1, f2, f3))
    old = gap
    for m, new in enumerate((a1, a2, a3, a4)):
        below = None
        for i in inner_layers(m):
            a = [old[n, i] for n in range(4)]
            f = fields[3 - m].all(i)
            for n, plane in enumerate(pull_gates(a, f)):
                new[n + 1, i] = plane
            if i not in inner_layers(m + 1):
                continue
            if below is None:
                below = wz[i - 1] * (a[0] - old[0, i - 1])
            above = wz[i] * (old[0, i + 1] - a[0])
            new[0, i] = pull_voltage(a, f) + (above - below) + cross(a[0], wx[i], wy[i])
            below = above
        old = new


def pull_kernel(
    starts, gap, before, p1, p2, p3, f1, f2, f3, b1, b2, b3, b4, wx, wy, wz, side, low, high,
    defect_out, gradient_out, work, defect, gradient, sems,
):
    for n in range(4):
        for i in range(DEEP):
            defect[n, i] = before[0, n, i] - starts[n, i]
    copies = [pltpu.make_async_copy(defect, defect_out.at[0], sems.at[DEEP])]
    copies[0].start()
    fields = forward_fields(starts, (p1, p2, p3), (f1, f2, f3))
    adjoints = [Fields(gap, None, 0, 0)] + [
        Fields(b, work.at[j], j + 1, j) for j, b in enumerate((b1, b2, b3))
    ]
    halo = [low[0], high[0]]
    first = [None, None]
    last = [None, None]
    for m in range(4):
        old = adjoints[m]
        outflow = [None, None]
        above = None
        for i in rim_layers(m + 1):
            a = old.all(i)
            f = fields[3 - m].all(i)
            if i == 0:
                below = outflow[0] = side[0, C_W01] * (a[0] - halo[0])
            elif above is not None:
                below = above
            else:
                below = wz[i - 1] * (a[0] - old.plane(0, i - 1))
            if i == DEEP - 1:
                above = side[1, C_W01] * (halo[1] - a[0])
                outflow[1] = -above
            else:
                above = wz[i] * (old.plane(0, i + 1) - a[0])
            fresh = [pull_voltage(a, f) + (above - below) + cross(a[0], wx[i], wy[i])]
            if i in inner_layers(m):
                if m == 3:
                    fresh += [b4[n, i] for n in (1, 2, 3)]
            else:
                fresh += pull_gates(a, f)
            if i == m and m < 3:
                above = None
            if m < 3:
                for n, plane in enumerate(fresh):
                    work[m, n, i] = plane
                continue
            for n, plane in enumerate(fresh):
                gradient[n, i] = plane - defect[n, i]
            copy = pltpu.make_async_copy(gradient.at[:, i], gradient_out.at[0, :, i], sems.at[i])
            copy.start()
            copies.append(copy)
        if m == 3:
            continue
        for n, msg in enumerate((low, high)):
            win, px, py = side[n, C_WIN], side[n, C_WX], side[n, C_WY]
            if m == 0:
                change = first[n] = outflow[n]
            else:
                d = last[n]
                rate = side[n, C_D2] if m == 1 else side[n, C_D1]
                change = d + cross(d, px, py) + (rate - win) * d + outflow[n]
                if m == 2:
                    change = change + (win * win + side[n, C_E]) * first[n]
            halo[n] = msg[m + 1] + change
            last[n] = change
    for copy in copies:
        copy.wait()


VM = pl.BlockSpec(memory_space=pltpu.VMEM)
SM = pl.BlockSpec(memory_space=pltpu.SMEM)
ANY = pl.BlockSpec(memory_space=pl.ANY)
HBM = pl.BlockSpec(memory_space=pltpu.HBM)


def f32(*shape):
    return jax.ShapeDtypeStruct(shape, jnp.float32)


def i32(*shape):
    return jax.ShapeDtypeStruct(shape, jnp.int32)


def call(kernel, name, ins, outs, scratch=(), out_spec=VM):
    return pl.pallas_call(
        kernel,
        name=name,
        in_specs=ins,
        out_specs=[out_spec] * len(outs),
        out_shape=outs,
        scratch_shapes=list(scratch),
        compiler_params=pltpu.CompilerParams(vmem_limit_bytes=28 * 1024 * 1024),
    )


def nearest(sections, slabs, pairs):
    return [
        ((k ^ 2) * slabs + source, k * slabs + target) for k in range(sections) for source, target in pairs
    ]


def body(starts, tissue, fibers, pacing, conductances):
    plane = (NX, NY)
    slab = (DEEP, *plane)
    fields = f32(4, *slab)
    slabs = lax.axis_size("slab")
    sections = lax.axis_size("tm")
    upward = [(i, i + 1) for i in range(slabs - 1)]
    downward = [(i + 1, i) for i in range(slabs - 1)]
    earlier = [((i + 1) % sections, i) for i in range(sections)]
    later = [(i, (i + 1) % sections) for i in range(sections)]
    flag = (lax.axis_index("tm") == 0).astype(jnp.float32).reshape(1)
    few = [pltpu.SMEM((4, 3), jnp.float32), pltpu.SemaphoreType.DMA((1,))]

    conductances, starts, tissue, fibers, pacing = (
        pltpu.with_memory_space_constraint(arg, pltpu.HBM)
        for arg in (conductances, starts, tissue, fibers, pacing)
    )
    up, down, up_tissue, down_tissue, own, tis, fib, pac = call(
        edge_kernel,
        "edge",
        [HBM, SM] + [HBM] * 4,
        [f32(7, *plane)] * 2 + [f32(3, *plane)] * 2 + [fields] + [i32(*slab)] * 3,
        [pltpu.SMEM((4, 3), jnp.float32), pltpu.SemaphoreType.DMA((5,))],
    )(conductances, flag, starts, tissue, fibers, pacing)
    low = lax.ppermute(up, "slab", upward)
    high = lax.ppermute(down, "slab", downward)
    low_tissue = lax.ppermute(up_tissue, ("tm", "slab"), nearest(sections, slabs, upward))
    high_tissue = lax.ppermute(down_tissue, ("tm", "slab"), nearest(sections, slabs, downward))
    following = lax.ppermute(own[None], "tm", earlier)
    wx, wy, wz, p1, p2, p3, p4 = call(
        ahead_kernel,
        "ahead",
        [HBM, SM] + [VM] * 4,
        [f32(*slab), f32(*slab), f32(DEEP - 1, *plane)] + [fields] * 4,
        few,
    )(conductances, flag, own, tis, fib, pac)
    f1, f2, f3, ends, side = call(
        forward_kernel,
        "forward",
        [HBM, SM] + [VM] * 15,
        [fields] * 4 + [f32(2, 7, *plane)],
        few,
    )(conductances, flag, own, tis, fib, pac, wx, wy, wz, p1, p2, p3, p4, low, high, low_tissue, high_tissue)
    before = lax.ppermute(ends[None], "tm", later)
    history = (own, p1, p2, p3, f1, f2, f3)
    gap, up, down = call(
        send_kernel, "send", [VM] * 12, [fields, f32(4, *plane), f32(4, *plane)]
    )(ends, following, *history, wx, wy, wz)
    low = lax.ppermute(up, "slab", upward)
    high = lax.ppermute(down, "slab", downward)
    inner = call(back_kernel, "back", [VM] * 11 + [ANY], [fields] * 4)(gap, *history, wx, wy, wz, up)
    defect, gradient = call(
        pull_kernel,
        "pull",
        [VM] * 19,
        [f32(1, 4, *slab)] * 2,
        [pltpu.VMEM((3, 4, *slab), jnp.float32)]
        + [pltpu.VMEM((4, *slab), jnp.float32)] * 2
        + [pltpu.SemaphoreType.DMA((DEEP + 1,))],
        ANY,
    )(own, gap, before, p1, p2, p3, f1, f2, f3, *inner, wx, wy, wz, side, low, high)
    return defect, gradient


def solution(mesh):
    spread = P("tm", None, "slab", None, None)
    placed = (spread, P("slab", None, None), P("slab", None, None), P("slab", None, None), P())
    return jax.shard_map(body, mesh=mesh, in_specs=placed, out_specs=(spread, spread), check_vma=False)
```

```python
import jax
import jax.numpy as jnp
from jax import lax
from jax.experimental import pallas as pl
from jax.experimental.pallas import tpu as pltpu
from jax.sharding import PartitionSpec as P

DEEP = 8
NX = 64
NY = 128
V0, P1, G1, G2, G3, Q2, Q3 = range(7)
FIB, TIS, WIN = range(3)
C_W01, C_WIN, C_WX, C_WY = range(4)
C_D2, C_E, C_D1 = range(3)
HALF_STEP = 0.15 * 0.5


def ahead(plane, axis):
    return pltpu.roll(plane, plane.shape[axis] - 1, axis)


def behind(plane, axis):
    return pltpu.roll(plane, 1, axis)


def sigma(cond, fiber, direction):
    summed = jnp.zeros(fiber.shape, jnp.float32)
    for c in range(4):
        summed = jnp.where(fiber == c, cond[c, direction], summed)
    return summed


def cross_weight(sig, share, axis):
    place = lax.broadcasted_iota(jnp.int32, sig.shape, axis)
    inner = jnp.where(place < sig.shape[axis] - 1, HALF_STEP, 0.0)
    return inner * (sig + ahead(sig, axis)) * (share * ahead(share, axis))


def face_weight(sig_a, share_a, sig_b, share_b):
    return HALF_STEP * (sig_a + sig_b) * (share_a * share_b)


def cross(v, wx, wy):
    fx = wx * (ahead(v, 0) - v)
    fy = wy * (ahead(v, 1) - v)
    return (fx - behind(fx, 0)) + (fy - behind(fy, 1))


def reaction(v, g1, g2, g3):
    return 0.3 * (g1 * g2) * (1.0 - v) - 0.15 * g3 * v


def tanhs(v):
    return jnp.tanh(4.0 * v - 0.8), jnp.tanh(2.0 - 4.0 * v), jnp.tanh(4.0 * v - 3.2)


def gates_next(v, g1, g2, g3):
    t1, t2, t3 = tanhs(v)
    return (
        0.7 * g1 + (0.15 + 0.15 * t1),
        0.9 * g2 + (0.05 + 0.05 * t2),
        0.97 * g3 + (0.015 + 0.015 * t3),
    )


def fetch(copies, sems):
    started = [pltpu.make_async_copy(src, dst, sems.at[n]) for n, (src, dst) in enumerate(copies)]
    for copy in started:
        copy.start()
    for copy in started:
        copy.wait()


def edge_kernel(
    cond_in, flag, starts_in, tissue_in, fibers_in, pacing_in,
    up, down, up_tissue, down_tissue, starts, tissue, fibers, pacing, cond, sems,
):
    fetch(
        [
            (starts_in.at[0], starts),
            (tissue_in, tissue),
            (fibers_in, fibers),
            (pacing_in, pacing),
            (cond_in, cond),
        ],
        sems,
    )
    for out, out_tissue, (b1, b2, b3, b4) in (
        (up, up_tissue, (7, 6, 5, 4)),
        (down, down_tissue, (0, 1, 2, 3)),
    ):
        share = [tissue[b].astype(jnp.float32) for b in (b1, b2, b3, b4)]
        sig0 = [sigma(cond, fibers[b], 0) for b in (b1, b2, b3, b4)]
        wz = [face_weight(sig0[i], share[i], sig0[i + 1], share[i + 1]) for i in range(3)]
        wx = [cross_weight(sigma(cond, fibers[b], 1), share[i], 0) for i, b in enumerate((b1, b2, b3))]
        wy = [cross_weight(sigma(cond, fibers[b], 2), share[i], 1) for i, b in enumerate((b1, b2, b3))]
        stim = [(0.6 * flag[0]) * pacing[b].astype(jnp.float32) for b in (b1, b2, b3)]
        v = [starts[0, b] for b in (b1, b2, b3, b4)]
        g = [[starts[n, b] for n in (1, 2, 3)] for b in (b1, b2, b3)]

        def own_step(i):
            total = v[i] + cross(v[i], wx[i], wy[i]) + reaction(v[i], *g[i]) + stim[i]
            total = total + wz[i] * (v[i + 1] - v[i])
            return total if i == 0 else total + wz[i - 1] * (v[i - 1] - v[i])

        out[V0] = v[0]
        out[P1] = own_step(0)
        gates = gates_next(v[0], *g[0])
        for n in range(3):
            out[G1 + n] = gates[n]
        v1_b2 = own_step(1)
        v1_b3 = own_step(2)
        out[Q2] = wz[0] * v1_b2 + stim[0]
        rest = v1_b2 + cross(v1_b2, wx[1], wy[1]) + reaction(v1_b2, *gates_next(v[1], *g[1])) + stim[1]
        rest = rest + wz[1] * (v1_b3 - v1_b2) - wz[0] * v1_b2
        out[Q3] = wz[0] * rest + stim[0]
        out_tissue[FIB] = fibers[b1].astype(jnp.float32)
        out_tissue[TIS] = share[0]
        out_tissue[WIN] = wz[0]


class Fields:
    def __init__(self, inner, outer, rim_voltage, rim_gate):
        self.refs = (inner, outer)
        self.rims = (rim_voltage, rim_gate)

    def plane(self, field, layer):
        rim = self.rims[0] if field == 0 else self.rims[1]
        inside = rim <= layer < DEEP - rim
        return self.refs[0 if inside else 1][field, layer]

    def all(self, layer):
        return [self.plane(n, layer) for n in range(4)]


def forward_fields(starts, inner, outer):
    return [Fields(starts, None, 0, 0)] + [Fields(inner[j - 1], outer[j - 1], j, j - 1) for j in (1, 2, 3)]


def inner_layers(rim):
    return range(rim, DEEP - rim)


def rim_layers(rim):
    return [i for i in range(DEEP) if not rim <= i < DEEP - rim]


def rim_kernel(cond_in, tissue, fibers, low_tissue, high_tissue, rim, cond, sems):
    fetch([(cond_in, cond)], sems)
    for n, (beside, own) in enumerate(((low_tissue, 0), (high_tissue, DEEP - 1))):
        fib, tis = beside[FIB], beside[TIS]
        rim[n, C_W01] = face_weight(
            sigma(cond, fib, 0), tis, sigma(cond, fibers[own], 0), tissue[own].astype(jnp.float32)
        )
        rim[n, C_WIN] = beside[WIN]
        rim[n, C_WX] = cross_weight(sigma(cond, fib, 1), tis, 0)
        rim[n, C_WY] = cross_weight(sigma(cond, fib, 2), tis, 1)


def ahead_kernel(cond_in, flag, starts, tissue, fibers, pacing, wx, wy, wz, f1, f2, f3, f4, cond, sems):
    fetch([(cond_in, cond)], sems)
    before = None
    for i in range(DEEP):
        share = tissue[i].astype(jnp.float32)
        sig0 = sigma(cond, fibers[i], 0)
        wx[i] = cross_weight(sigma(cond, fibers[i], 1), share, 0)
        wy[i] = cross_weight(sigma(cond, fibers[i], 2), share, 1)
        if i:
            wz[i - 1] = face_weight(*before, sig0, share)
        before = (sig0, share)
    old = starts
    for step, new in enumerate((f1, f2, f3, f4)):
        below = None
        for i in inner_layers(step):
            v, *g = [old[n, i] for n in range(4)]
            for n, gate in enumerate(gates_next(v, *g)):
                new[n + 1, i] = gate
            if step == 0:
                low, high = i > 0, i < DEEP - 1
            else:
                low = high = step + 1 <= i < DEEP - step - 1
            if not (low or high):
                continue
            total = v + cross(v, wx[i], wy[i]) + reaction(v, *g)
            total = total + (0.6 * flag[0]) * pacing[i].astype(jnp.float32)
            if low:
                total = total - (wz[i - 1] * (v - old[0, i - 1]) if below is None else below)
            below = None
            if high:
                below = wz[i] * (old[0, i + 1] - v)
                total = total + below
            new[0, i] = total
        old = new


def forward_kernel(
    flag, starts, pacing, wx, wy, wz, rim, p1, p2, p3, p4, low, high,
    f1, f2, f3, f4, side,
):
    halo = []
    for n, (msg, own) in enumerate(((low, 0), (high, DEEP - 1))):
        inflow = rim[n, C_W01] * (msg[V0] - starts[0, own])
        f1[0, own] = p1[0, own] + inflow
        halo.append(msg[P1] - inflow)
        side[n, C_D1] = halo[n]
    fields = forward_fields(starts, (p1, p2, p3), (f1, f2, f3))
    for n in range(1, 4):
        for i in inner_layers(3):
            f4[n, i] = p4[n, i]
    for step in (1, 2, 3):
        old = fields[step]
        new = (f1, f2, f3, f4)[step]
        outflow = [None, None]
        above = None
        for i in rim_layers(step + 1):
            v, *g = old.all(i)
            if i not in inner_layers(step):
                for n, gate in enumerate(gates_next(v, *g)):
                    new[n + 1, i] = gate
            if i == 0:
                below = outflow[0] = rim[0, C_W01] * (v - halo[0])
            elif above is not None:
                below = above
            else:
                below = wz[i - 1] * (v - old.plane(0, i - 1))
            if i == DEEP - 1:
                above = rim[1, C_W01] * (halo[1] - v)
                outflow[1] = -above
            else:
                above = wz[i] * (old.plane(0, i + 1) - v)
            total = v + (above - below) + cross(v, wx[i], wy[i]) + reaction(v, *g)
            new[0, i] = total + (0.6 * flag[0]) * pacing[i].astype(jnp.float32)
            if i == step and step < 3:
                above = None
        if step == 3:
            continue
        for n, msg in enumerate((low, high)):
            v = halo[n]
            win = rim[n, C_WIN]
            g = [msg[G1], msg[G2], msg[G3]]
            if step == 1:
                extra = msg[Q2]
            else:
                v1 = side[n, C_D1]
                g1 = g
                g = gates_next(v1, *g1)
                extra = msg[Q3] + win * win * v1
                t1, t2, t3 = tanhs(v1)
                side[n, C_D2] = -0.3 * (g[0] * g[1]) - 0.15 * g[2]
                side[n, C_D1] = -0.3 * (g1[0] * g1[1]) - 0.15 * g1[2]
                side[n, C_E] = (
                    0.6 * (1.0 - t1 * t1) * (0.3 * g[1] * (1.0 - v))
                    - 0.2 * (1.0 - t2 * t2) * (0.3 * g[0] * (1.0 - v))
                    - 0.06 * (1.0 - t3 * t3) * (0.15 * v)
                )
            total = v + cross(v, rim[n, C_WX], rim[n, C_WY]) + reaction(v, *g)
            halo[n] = total + (extra - win * v) + outflow[n]


def pull_gates(a, f):
    av, a1, a2, a3 = a
    v, g1, g2, g3 = f
    rest = 0.3 * (1.0 - v) * av
    return 0.7 * a1 + g2 * rest, 0.9 * a2 + g1 * rest, 0.97 * a3 - 0.15 * v * av


def pull_voltage(a, f):
    av, a1, a2, a3 = a
    v, g1, g2, g3 = f
    t1, t2, t3 = tanhs(v)
    total = av * (1.0 - 0.3 * (g1 * g2) - 0.15 * g3)
    total = total + 0.6 * (1.0 - t1 * t1) * a1 - 0.2 * (1.0 - t2 * t2) * a2
    return total + 0.06 * (1.0 - t3 * t3) * a3


def send_kernel(ends, following, starts, p1, p2, p3, f1, f2, f3, wx, wy, wz, gap, up, down):
    fields = forward_fields(starts, (p1, p2, p3), (f1, f2, f3))
    for n in range(4):
        for i in range(DEEP):
            gap[n, i] = ends[n, i] - following[0, n, i]
    for out, (b1, sign) in ((up, (7, -1)), (down, (0, 1))):
        layers = [b1 + sign * d for d in range(4)]
        a = [[gap[n, b] for n in range(4)] for b in layers]
        out[0] = a[0][0]
        for m in range(3):
            fresh = []
            outer = None
            for d in range(3 - m):
                b = layers[d]
                f = fields[3 - m].all(b)
                face = wz[b - 1] if sign < 0 else wz[b]
                inner = face * (a[d + 1][0] - a[d][0])
                total = pull_voltage(a[d], f) + cross(a[d][0], wx[b], wy[b]) + inner
                if outer is not None:
                    total = total - outer
                fresh.append([total, *pull_gates(a[d], f)])
                outer = inner
            a = fresh
            out[m + 1] = a[0][0]


def back_kernel(gap, starts, p1, p2, p3, f1, f2, f3, wx, wy, wz, gate, a1, a2, a3, a4):
    fields = forward_fields(starts, (p1, p2, p3), (f1, f2, f3))
    old = gap
    for m, new in enumerate((a1, a2, a3, a4)):
        below = None
        for i in inner_layers(m):
            a = [old[n, i] for n in range(4)]
            f = fields[3 - m].all(i)
            for n, plane in enumerate(pull_gates(a, f)):
                new[n + 1, i] = plane
            if i not in inner_layers(m + 1):
                continue
            if below is None:
                below = wz[i - 1] * (a[0] - old[0, i - 1])
            above = wz[i] * (old[0, i + 1] - a[0])
            new[0, i] = pull_voltage(a, f) + (above - below) + cross(a[0], wx[i], wy[i])
            below = above
        old = new


def defect_kernel(starts, before, defect_out, defect, sems):
    copies = []
    for n in range(4):
        for i in range(DEEP):
            defect[n, i] = before[0, n, i] - starts[n, i]
        copies.append(pltpu.make_async_copy(defect.at[n], defect_out.at[0, n], sems.at[n]))
        copies[n].start()
    for copy in copies:
        copy.wait()


def pull_kernel(
    starts, gap, defect, p1, p2, p3, f1, f2, f3, b1, b2, b3, b4, wx, wy, wz, rim, side, low, high,
    gradient_out, work, gradient, sems,
):
    copies = []
    fields = forward_fields(starts, (p1, p2, p3), (f1, f2, f3))
    adjoints = [Fields(gap, None, 0, 0)] + [
        Fields(b, work.at[j], j + 1, j) for j, b in enumerate((b1, b2, b3))
    ]
    halo = [low[0], high[0]]
    first = [None, None]
    last = [None, None]
    for m in range(4):
        old = adjoints[m]
        outflow = [None, None]
        above = None
        for i in rim_layers(m + 1):
            a = old.all(i)
            f = fields[3 - m].all(i)
            if i == 0:
                below = outflow[0] = rim[0, C_W01] * (a[0] - halo[0])
            elif above is not None:
                below = above
            else:
                below = wz[i - 1] * (a[0] - old.plane(0, i - 1))
            if i == DEEP - 1:
                above = rim[1, C_W01] * (halo[1] - a[0])
                outflow[1] = -above
            else:
                above = wz[i] * (old.plane(0, i + 1) - a[0])
            fresh = [pull_voltage(a, f) + (above - below) + cross(a[0], wx[i], wy[i])]
            if i in inner_layers(m):
                if m == 3:
                    fresh += [b4[n, i] for n in (1, 2, 3)]
            else:
                fresh += pull_gates(a, f)
            if i == m and m < 3:
                above = None
            if m < 3:
                for n, plane in enumerate(fresh):
                    work[m, n, i] = plane
                continue
            for n, plane in enumerate(fresh):
                gradient[n, i] = plane - defect[n, i]
            copy = pltpu.make_async_copy(gradient.at[:, i], gradient_out.at[0, :, i], sems.at[i])
            copy.start()
            copies.append(copy)
        if m == 3:
            continue
        for n, msg in enumerate((low, high)):
            win, px, py = rim[n, C_WIN], rim[n, C_WX], rim[n, C_WY]
            if m == 0:
                change = first[n] = outflow[n]
            else:
                d = last[n]
                rate = side[n, C_D2] if m == 1 else side[n, C_D1]
                change = d + cross(d, px, py) + (rate - win) * d + outflow[n]
                if m == 2:
                    change = change + (win * win + side[n, C_E]) * first[n]
            halo[n] = msg[m + 1] + change
            last[n] = change
    for copy in copies:
        copy.wait()


VM = pl.BlockSpec(memory_space=pltpu.VMEM)
SM = pl.BlockSpec(memory_space=pltpu.SMEM)
ANY = pl.BlockSpec(memory_space=pl.ANY)
HBM = pl.BlockSpec(memory_space=pltpu.HBM)


def f32(*shape):
    return jax.ShapeDtypeStruct(shape, jnp.float32)


def i32(*shape):
    return jax.ShapeDtypeStruct(shape, jnp.int32)


def call(kernel, name, ins, outs, scratch=(), out_specs=None):
    return pl.pallas_call(
        kernel,
        name=name,
        in_specs=ins,
        out_specs=out_specs or [VM] * len(outs),
        out_shape=outs,
        scratch_shapes=list(scratch),
        compiler_params=pltpu.CompilerParams(vmem_limit_bytes=28 * 1024 * 1024),
    )


def nearest(sections, slabs, pairs):
    return [
        ((k ^ 2) * slabs + source, k * slabs + target) for k in range(sections) for source, target in pairs
    ]


def body(starts, tissue, fibers, pacing, conductances):
    plane = (NX, NY)
    slab = (DEEP, *plane)
    fields = f32(4, *slab)
    slabs = lax.axis_size("slab")
    sections = lax.axis_size("tm")
    upward = [(i, i + 1) for i in range(slabs - 1)]
    downward = [(i + 1, i) for i in range(slabs - 1)]
    earlier = [((i + 1) % sections, i) for i in range(sections)]
    later = [(i, (i + 1) % sections) for i in range(sections)]
    flag = (lax.axis_index("tm") == 0).astype(jnp.float32).reshape(1)

    conductances, starts, tissue, fibers, pacing = (
        pltpu.with_memory_space_constraint(arg, pltpu.HBM)
        for arg in (conductances, starts, tissue, fibers, pacing)
    )
    up, down, up_tissue, down_tissue, own, tis, fib, pac = call(
        edge_kernel,
        "edge",
        [HBM, SM] + [HBM] * 4,
        [f32(7, *plane)] * 2 + [f32(3, *plane)] * 2 + [fields] + [i32(*slab)] * 3,
        [pltpu.SMEM((4, 3), jnp.float32), pltpu.SemaphoreType.DMA((5,))],
    )(conductances, flag, starts, tissue, fibers, pacing)
    low = lax.ppermute(up, "slab", upward)
    high = lax.ppermute(down, "slab", downward)
    low_tissue = lax.ppermute(up_tissue, ("tm", "slab"), nearest(sections, slabs, upward))
    high_tissue = lax.ppermute(down_tissue, ("tm", "slab"), nearest(sections, slabs, downward))
    following = lax.ppermute(own[None], "tm", earlier)
    few = [pltpu.SMEM((4, 3), jnp.float32), pltpu.SemaphoreType.DMA((1,))]
    wx, wy, wz, p1, p2, p3, p4 = call(
        ahead_kernel,
        "ahead",
        [HBM, SM] + [VM] * 4,
        [f32(*slab), f32(*slab), f32(DEEP - 1, *plane)] + [fields] * 4,
        few,
    )(conductances, flag, own, tis, fib, pac)
    rim = call(rim_kernel, "rim", [HBM] + [VM] * 4, [f32(2, 4, *plane)], few)(
        conductances, tis, fib, low_tissue, high_tissue
    )[0]
    f1, f2, f3, ends, side = call(
        forward_kernel,
        "forward",
        [SM] + [VM] * 12,
        [fields] * 4 + [f32(2, 3, *plane)],
    )(flag, own, pac, wx, wy, wz, rim, p1, p2, p3, p4, low, high)
    before = lax.ppermute(ends[None], "tm", later)
    history = (own, p1, p2, p3, f1, f2, f3)
    gap, up, down = call(
        send_kernel, "send", [VM] * 12, [fields, f32(4, *plane), f32(4, *plane)]
    )(ends, following, *history, wx, wy, wz)
    low = lax.ppermute(up, "slab", upward)
    high = lax.ppermute(down, "slab", downward)
    inner = call(back_kernel, "back", [VM] * 11 + [ANY], [fields] * 4)(gap, *history, wx, wy, wz, up)
    defect, kept = call(
        defect_kernel,
        "defect",
        [VM] * 2,
        [f32(1, 4, *slab), fields],
        [pltpu.SemaphoreType.DMA((4,))],
        [ANY, VM],
    )(own, before)
    gradient = call(
        pull_kernel,
        "pull",
        [VM] * 20,
        [f32(1, 4, *slab)],
        [
            pltpu.VMEM((3, 4, *slab), jnp.float32),
            pltpu.VMEM((4, *slab), jnp.float32),
            pltpu.SemaphoreType.DMA((DEEP,)),
        ],
        [ANY],
    )(own, gap, kept, p1, p2, p3, f1, f2, f3, *inner, wx, wy, wz, rim, side, low, high)[0]
    return defect, gradient


def solution(mesh):
    spread = P("tm", None, "slab", None, None)
    placed = (spread, P("slab", None, None), P("slab", None, None), P("slab", None, None), P())
    return jax.shard_map(body, mesh=mesh, in_specs=placed, out_specs=(spread, spread), check_vma=False)
```

```python
import jax
import jax.numpy as jnp
from jax import lax
from jax.experimental import pallas as pl
from jax.experimental.pallas import tpu as pltpu
from jax.sharding import PartitionSpec as P

DEEP = 8
NX = 64
NY = 128
V0, P1, G1, G2, G3, Q2, Q3 = range(7)
FIB, TIS, WIN = range(3)
C_W01, C_WIN, C_WX, C_WY = range(4)
C_D2, C_E, C_D1 = range(3)
HALF_STEP = 0.15 * 0.5


def ahead(plane, axis):
    return pltpu.roll(plane, plane.shape[axis] - 1, axis)


def behind(plane, axis):
    return pltpu.roll(plane, 1, axis)


def sigma(cond, fiber, direction):
    summed = jnp.zeros(fiber.shape, jnp.float32)
    for c in range(4):
        summed = jnp.where(fiber == c, cond[c, direction], summed)
    return summed


def cross_weight(sig, share, axis):
    place = lax.broadcasted_iota(jnp.int32, sig.shape, axis)
    inner = jnp.where(place < sig.shape[axis] - 1, HALF_STEP, 0.0)
    return inner * (sig + ahead(sig, axis)) * (share * ahead(share, axis))


def face_weight(sig_a, share_a, sig_b, share_b):
    return HALF_STEP * (sig_a + sig_b) * (share_a * share_b)


def cross(v, wx, wy):
    fx = wx * (ahead(v, 0) - v)
    fy = wy * (ahead(v, 1) - v)
    return (fx - behind(fx, 0)) + (fy - behind(fy, 1))


def reaction(v, g1, g2, g3):
    return 0.3 * (g1 * g2) * (1.0 - v) - 0.15 * g3 * v


def tanhs(v):
    return jnp.tanh(4.0 * v - 0.8), jnp.tanh(2.0 - 4.0 * v), jnp.tanh(4.0 * v - 3.2)


def gates_next(v, g1, g2, g3):
    t1, t2, t3 = tanhs(v)
    return (
        0.7 * g1 + (0.15 + 0.15 * t1),
        0.9 * g2 + (0.05 + 0.05 * t2),
        0.97 * g3 + (0.015 + 0.015 * t3),
    )


def fetch(copies, sems):
    started = [pltpu.make_async_copy(src, dst, sems.at[n]) for n, (src, dst) in enumerate(copies)]
    for copy in started:
        copy.start()
    for copy in started:
        copy.wait()


def edge_kernel(
    cond_in, flag, starts_in, tissue_in, fibers_in, pacing_in,
    up, down, up_tissue, down_tissue, starts, tissue, fibers, pacing, cond, sems,
):
    fetch(
        [
            (starts_in.at[0], starts),
            (tissue_in, tissue),
            (fibers_in, fibers),
            (pacing_in, pacing),
            (cond_in, cond),
        ],
        sems,
    )
    for out, out_tissue, (b1, b2, b3, b4) in (
        (up, up_tissue, (7, 6, 5, 4)),
        (down, down_tissue, (0, 1, 2, 3)),
    ):
        share = [tissue[b].astype(jnp.float32) for b in (b1, b2, b3, b4)]
        sig0 = [sigma(cond, fibers[b], 0) for b in (b1, b2, b3, b4)]
        wz = [face_weight(sig0[i], share[i], sig0[i + 1], share[i + 1]) for i in range(3)]
        wx = [cross_weight(sigma(cond, fibers[b], 1), share[i], 0) for i, b in enumerate((b1, b2, b3))]
        wy = [cross_weight(sigma(cond, fibers[b], 2), share[i], 1) for i, b in enumerate((b1, b2, b3))]
        stim = [(0.6 * flag[0]) * pacing[b].astype(jnp.float32) for b in (b1, b2, b3)]
        v = [starts[0, b] for b in (b1, b2, b3, b4)]
        g = [[starts[n, b] for n in (1, 2, 3)] for b in (b1, b2, b3)]

        def own_step(i):
            total = v[i] + cross(v[i], wx[i], wy[i]) + reaction(v[i], *g[i]) + stim[i]
            total = total + wz[i] * (v[i + 1] - v[i])
            return total if i == 0 else total + wz[i - 1] * (v[i - 1] - v[i])

        out[V0] = v[0]
        out[P1] = own_step(0)
        gates = gates_next(v[0], *g[0])
        for n in range(3):
            out[G1 + n] = gates[n]
        v1_b2 = own_step(1)
        v1_b3 = own_step(2)
        out[Q2] = wz[0] * v1_b2 + stim[0]
        rest = v1_b2 + cross(v1_b2, wx[1], wy[1]) + reaction(v1_b2, *gates_next(v[1], *g[1])) + stim[1]
        rest = rest + wz[1] * (v1_b3 - v1_b2) - wz[0] * v1_b2
        out[Q3] = wz[0] * rest + stim[0]
        out_tissue[FIB] = fibers[b1].astype(jnp.float32)
        out_tissue[TIS] = share[0]
        out_tissue[WIN] = wz[0]


class Fields:
    def __init__(self, inner, outer, rim_voltage, rim_gate):
        self.refs = (inner, outer)
        self.rims = (rim_voltage, rim_gate)

    def plane(self, field, layer):
        rim = self.rims[0] if field == 0 else self.rims[1]
        inside = rim <= layer < DEEP - rim
        return self.refs[0 if inside else 1][field, layer]

    def all(self, layer):
        return [self.plane(n, layer) for n in range(4)]


def forward_fields(starts, inner, outer):
    return [Fields(starts, None, 0, 0)] + [Fields(inner[j - 1], outer[j - 1], j, j - 1) for j in (1, 2, 3)]


def inner_layers(rim):
    return range(rim, DEEP - rim)


def rim_layers(rim):
    return [i for i in range(DEEP) if not rim <= i < DEEP - rim]


def rim_kernel(cond_in, tissue, fibers, low_tissue, high_tissue, rim, cond, sems):
    fetch([(cond_in, cond)], sems)
    for n, (beside, own) in enumerate(((low_tissue, 0), (high_tissue, DEEP - 1))):
        fib, tis = beside[FIB], beside[TIS]
        rim[n, C_W01] = face_weight(
            sigma(cond, fib, 0), tis, sigma(cond, fibers[own], 0), tissue[own].astype(jnp.float32)
        )
        rim[n, C_WIN] = beside[WIN]
        rim[n, C_WX] = cross_weight(sigma(cond, fib, 1), tis, 0)
        rim[n, C_WY] = cross_weight(sigma(cond, fib, 2), tis, 1)


def ahead_kernel(cond_in, flag, starts, tissue, fibers, pacing, wx, wy, wz, f1, f2, f3, f4, cond, sems):
    fetch([(cond_in, cond)], sems)
    before = None
    for i in range(DEEP):
        share = tissue[i].astype(jnp.float32)
        sig0 = sigma(cond, fibers[i], 0)
        wx[i] = cross_weight(sigma(cond, fibers[i], 1), share, 0)
        wy[i] = cross_weight(sigma(cond, fibers[i], 2), share, 1)
        if i:
            wz[i - 1] = face_weight(*before, sig0, share)
        before = (sig0, share)
    old = starts
    for step, new in enumerate((f1, f2, f3, f4)):
        below = None
        for i in inner_layers(step):
            v, *g = [old[n, i] for n in range(4)]
            for n, gate in enumerate(gates_next(v, *g)):
                new[n + 1, i] = gate
            if step == 0:
                low, high = i > 0, i < DEEP - 1
            else:
                low = high = step + 1 <= i < DEEP - step - 1
            if not (low or high):
                continue
            total = v + cross(v, wx[i], wy[i]) + reaction(v, *g)
            total = total + (0.6 * flag[0]) * pacing[i].astype(jnp.float32)
            if low:
                total = total - (wz[i - 1] * (v - old[0, i - 1]) if below is None else below)
            below = None
            if high:
                below = wz[i] * (old[0, i + 1] - v)
                total = total + below
            new[0, i] = total
        old = new


def forward_kernel(
    flag, starts, pacing, wx, wy, wz, rim, p1, p2, p3, p4, high, low,
    f1, f2, f3, f4, side,
):
    halo = []
    for n, (msg, own) in enumerate(((low, 0), (high, DEEP - 1))):
        inflow = rim[n, C_W01] * (msg[V0] - starts[0, own])
        f1[0, own] = p1[0, own] + inflow
        halo.append(msg[P1] - inflow)
        side[n, C_D1] = halo[n]
    fields = forward_fields(starts, (p1, p2, p3), (f1, f2, f3))
    for n in range(1, 4):
        for i in inner_layers(3):
            f4[n, i] = p4[n, i]
    for step in (1, 2, 3):
        old = fields[step]
        new = (f1, f2, f3, f4)[step]
        outflow = [None, None]
        above = None
        for i in rim_layers(step + 1):
            v, *g = old.all(i)
            if i not in inner_layers(step):
                for n, gate in enumerate(gates_next(v, *g)):
                    new[n + 1, i] = gate
            if i == 0:
                below = outflow[0] = rim[0, C_W01] * (v - halo[0])
            elif above is not None:
                below = above
            else:
                below = wz[i - 1] * (v - old.plane(0, i - 1))
            if i == DEEP - 1:
                above = rim[1, C_W01] * (halo[1] - v)
                outflow[1] = -above
            else:
                above = wz[i] * (old.plane(0, i + 1) - v)
            total = v + (above - below) + cross(v, wx[i], wy[i]) + reaction(v, *g)
            new[0, i] = total + (0.6 * flag[0]) * pacing[i].astype(jnp.float32)
            if i == step and step < 3:
                above = None
        if step == 3:
            continue
        for n, msg in enumerate((low, high)):
            v = halo[n]
            win = rim[n, C_WIN]
            g = [msg[G1], msg[G2], msg[G3]]
            if step == 1:
                extra = msg[Q2]
            else:
                v1 = side[n, C_D1]
                g1 = g
                g = gates_next(v1, *g1)
                extra = msg[Q3] + win * win * v1
                t1, t2, t3 = tanhs(v1)
                side[n, C_D2] = -0.3 * (g[0] * g[1]) - 0.15 * g[2]
                side[n, C_D1] = -0.3 * (g1[0] * g1[1]) - 0.15 * g1[2]
                side[n, C_E] = (
                    0.6 * (1.0 - t1 * t1) * (0.3 * g[1] * (1.0 - v))
                    - 0.2 * (1.0 - t2 * t2) * (0.3 * g[0] * (1.0 - v))
                    - 0.06 * (1.0 - t3 * t3) * (0.15 * v)
                )
            total = v + cross(v, rim[n, C_WX], rim[n, C_WY]) + reaction(v, *g)
            halo[n] = total + (extra - win * v) + outflow[n]


def pull_gates(a, f):
    av, a1, a2, a3 = a
    v, g1, g2, g3 = f
    rest = 0.3 * (1.0 - v) * av
    return 0.7 * a1 + g2 * rest, 0.9 * a2 + g1 * rest, 0.97 * a3 - 0.15 * v * av


def pull_voltage(a, f):
    av, a1, a2, a3 = a
    v, g1, g2, g3 = f
    t1, t2, t3 = tanhs(v)
    total = av * (1.0 - 0.3 * (g1 * g2) - 0.15 * g3)
    total = total + 0.6 * (1.0 - t1 * t1) * a1 - 0.2 * (1.0 - t2 * t2) * a2
    return total + 0.06 * (1.0 - t3 * t3) * a3


def send_kernel(ends, following, starts, p1, p2, p3, f1, f2, f3, wx, wy, wz, gap, up, down):
    fields = forward_fields(starts, (p1, p2, p3), (f1, f2, f3))
    for n in range(4):
        for i in range(DEEP):
            gap[n, i] = ends[n, i] - following[0, n, i]
    for out, (b1, sign) in ((up, (7, -1)), (down, (0, 1))):
        layers = [b1 + sign * d for d in range(4)]
        a = [[gap[n, b] for n in range(4)] for b in layers]
        out[0] = a[0][0]
        for m in range(3):
            fresh = []
            outer = None
            for d in range(3 - m):
                b = layers[d]
                f = fields[3 - m].all(b)
                face = wz[b - 1] if sign < 0 else wz[b]
                inner = face * (a[d + 1][0] - a[d][0])
                total = pull_voltage(a[d], f) + cross(a[d][0], wx[b], wy[b]) + inner
                if outer is not None:
                    total = total - outer
                fresh.append([total, *pull_gates(a[d], f)])
                outer = inner
            a = fresh
            out[m + 1] = a[0][0]


def back_kernel(gap, starts, p1, p2, p3, f1, f2, f3, wx, wy, wz, gate, a1, a2, a3, a4):
    fields = forward_fields(starts, (p1, p2, p3), (f1, f2, f3))
    old = gap
    for m, new in enumerate((a1, a2, a3, a4)):
        below = None
        for i in inner_layers(m):
            a = [old[n, i] for n in range(4)]
            f = fields[3 - m].all(i)
            for n, plane in enumerate(pull_gates(a, f)):
                new[n + 1, i] = plane
            if i not in inner_layers(m + 1):
                continue
            if below is None:
                below = wz[i - 1] * (a[0] - old[0, i - 1])
            above = wz[i] * (old[0, i + 1] - a[0])
            new[0, i] = pull_voltage(a, f) + (above - below) + cross(a[0], wx[i], wy[i])
            below = above
        old = new


def defect_kernel(starts, before, defect_out, defect, sems):
    copies = []
    for n in range(4):
        for i in range(DEEP):
            defect[n, i] = before[0, n, i] - starts[n, i]
        copies.append(pltpu.make_async_copy(defect.at[n], defect_out.at[0, n], sems.at[n]))
        copies[n].start()
    for copy in copies:
        copy.wait()


def pull_kernel(
    starts, gap, defect, p1, p2, p3, f1, f2, f3, b1, b2, b3, b4, wx, wy, wz, rim, side, low, high,
    gradient_out, work, gradient, sems,
):
    copies = []
    fields = forward_fields(starts, (p1, p2, p3), (f1, f2, f3))
    adjoints = [Fields(gap, None, 0, 0)] + [
        Fields(b, work.at[j], j + 1, j) for j, b in enumerate((b1, b2, b3))
    ]
    halo = [low[0], high[0]]
    first = [None, None]
    last = [None, None]
    for m in range(4):
        old = adjoints[m]
        outflow = [None, None]
        above = None
        for i in rim_layers(m + 1):
            a = old.all(i)
            f = fields[3 - m].all(i)
            if i == 0:
                below = outflow[0] = rim[0, C_W01] * (a[0] - halo[0])
            elif above is not None:
                below = above
            else:
                below = wz[i - 1] * (a[0] - old.plane(0, i - 1))
            if i == DEEP - 1:
                above = rim[1, C_W01] * (halo[1] - a[0])
                outflow[1] = -above
            else:
                above = wz[i] * (old.plane(0, i + 1) - a[0])
            fresh = [pull_voltage(a, f) + (above - below) + cross(a[0], wx[i], wy[i])]
            if i in inner_layers(m):
                if m == 3:
                    fresh += [b4[n, i] for n in (1, 2, 3)]
            else:
                fresh += pull_gates(a, f)
            if i == m and m < 3:
                above = None
            if m < 3:
                for n, plane in enumerate(fresh):
                    work[m, n, i] = plane
                continue
            for n, plane in enumerate(fresh):
                gradient[n, i] = plane - defect[n, i]
            copy = pltpu.make_async_copy(gradient.at[:, i], gradient_out.at[0, :, i], sems.at[i])
            copy.start()
            copies.append(copy)
        if m == 3:
            continue
        for n, msg in enumerate((low, high)):
            win, px, py = rim[n, C_WIN], rim[n, C_WX], rim[n, C_WY]
            if m == 0:
                change = first[n] = outflow[n]
            else:
                d = last[n]
                rate = side[n, C_D2] if m == 1 else side[n, C_D1]
                change = d + cross(d, px, py) + (rate - win) * d + outflow[n]
                if m == 2:
                    change = change + (win * win + side[n, C_E]) * first[n]
            halo[n] = msg[m + 1] + change
            last[n] = change
    for copy in copies:
        copy.wait()


VM = pl.BlockSpec(memory_space=pltpu.VMEM)
SM = pl.BlockSpec(memory_space=pltpu.SMEM)
ANY = pl.BlockSpec(memory_space=pl.ANY)
HBM = pl.BlockSpec(memory_space=pltpu.HBM)


def f32(*shape):
    return jax.ShapeDtypeStruct(shape, jnp.float32)


def i32(*shape):
    return jax.ShapeDtypeStruct(shape, jnp.int32)


def call(kernel, name, ins, outs, scratch=(), out_specs=None):
    return pl.pallas_call(
        kernel,
        name=name,
        in_specs=ins,
        out_specs=out_specs or [VM] * len(outs),
        out_shape=outs,
        scratch_shapes=list(scratch),
        compiler_params=pltpu.CompilerParams(vmem_limit_bytes=28 * 1024 * 1024),
    )


def nearest(sections, slabs, pairs):
    return [
        ((k ^ 2) * slabs + source, k * slabs + target) for k in range(sections) for source, target in pairs
    ]


def body(starts, tissue, fibers, pacing, conductances):
    plane = (NX, NY)
    slab = (DEEP, *plane)
    fields = f32(4, *slab)
    slabs = lax.axis_size("slab")
    sections = lax.axis_size("tm")
    upward = [(i, i + 1) for i in range(slabs - 1)]
    downward = [(i + 1, i) for i in range(slabs - 1)]
    earlier = [((i + 1) % sections, i) for i in range(sections)]
    later = [(i, (i + 1) % sections) for i in range(sections)]
    flag = (lax.axis_index("tm") == 0).astype(jnp.float32).reshape(1)

    conductances, starts, tissue, fibers, pacing = (
        pltpu.with_memory_space_constraint(arg, pltpu.HBM)
        for arg in (conductances, starts, tissue, fibers, pacing)
    )
    up, down, up_tissue, down_tissue, own, tis, fib, pac = call(
        edge_kernel,
        "edge",
        [HBM, SM] + [HBM] * 4,
        [f32(7, *plane)] * 2 + [f32(3, *plane)] * 2 + [fields] + [i32(*slab)] * 3,
        [pltpu.SMEM((4, 3), jnp.float32), pltpu.SemaphoreType.DMA((5,))],
    )(conductances, flag, starts, tissue, fibers, pacing)
    high = lax.ppermute(down, "slab", downward)
    low = lax.ppermute(up, "slab", upward)
    low_tissue = lax.ppermute(up_tissue, ("tm", "slab"), nearest(sections, slabs, upward))
    high_tissue = lax.ppermute(down_tissue, ("tm", "slab"), nearest(sections, slabs, downward))
    following = lax.ppermute(own[None], "tm", earlier)
    few = [pltpu.SMEM((4, 3), jnp.float32), pltpu.SemaphoreType.DMA((1,))]
    wx, wy, wz, p1, p2, p3, p4 = call(
        ahead_kernel,
        "ahead",
        [HBM, SM] + [VM] * 4,
        [f32(*slab), f32(*slab), f32(DEEP - 1, *plane)] + [fields] * 4,
        few,
    )(conductances, flag, own, tis, fib, pac)
    rim = call(rim_kernel, "rim", [HBM] + [VM] * 4, [f32(2, 4, *plane)], few)(
        conductances, tis, fib, low_tissue, high_tissue
    )[0]
    f1, f2, f3, ends, side = call(
        forward_kernel,
        "forward",
        [SM] + [VM] * 12,
        [fields] * 4 + [f32(2, 3, *plane)],
    )(flag, own, pac, wx, wy, wz, rim, p1, p2, p3, p4, high, low)
    before = lax.ppermute(ends[None], "tm", later)
    history = (own, p1, p2, p3, f1, f2, f3)
    gap, up, down = call(
        send_kernel, "send", [VM] * 12, [fields, f32(4, *plane), f32(4, *plane)]
    )(ends, following, *history, wx, wy, wz)
    low = lax.ppermute(up, "slab", upward)
    high = lax.ppermute(down, "slab", downward)
    inner = call(back_kernel, "back", [VM] * 11 + [ANY], [fields] * 4)(gap, *history, wx, wy, wz, up)
    defect, kept = call(
        defect_kernel,
        "defect",
        [VM] * 2,
        [f32(1, 4, *slab), fields],
        [pltpu.SemaphoreType.DMA((4,))],
        [ANY, VM],
    )(own, before)
    gradient = call(
        pull_kernel,
        "pull",
        [VM] * 20,
        [f32(1, 4, *slab)],
        [
            pltpu.VMEM((3, 4, *slab), jnp.float32),
            pltpu.VMEM((4, *slab), jnp.float32),
            pltpu.SemaphoreType.DMA((DEEP,)),
        ],
        [ANY],
    )(own, gap, kept, p1, p2, p3, f1, f2, f3, *inner, wx, wy, wz, rim, side, low, high)[0]
    return defect, gradient


def solution(mesh):
    spread = P("tm", None, "slab", None, None)
    placed = (spread, P("slab", None, None), P("slab", None, None), P("slab", None, None), P())
    return jax.shard_map(body, mesh=mesh, in_specs=placed, out_specs=(spread, spread), check_vma=False)
```

```python
import jax
import jax.numpy as jnp
from jax import lax
from jax.experimental import pallas as pl
from jax.experimental.pallas import tpu as pltpu
from jax.sharding import PartitionSpec as P

DEEP = 8
NX = 64
NY = 128
V0, P1, G1, G2, G3, Q2, Q3 = range(7)
FIB, TIS, WIN = range(3)
C_W01, C_WIN, C_WX, C_WY = range(4)
C_D2, C_E, C_D1 = range(3)
HALF_STEP = 0.15 * 0.5


def ahead(plane, axis):
    return pltpu.roll(plane, plane.shape[axis] - 1, axis)


def behind(plane, axis):
    return pltpu.roll(plane, 1, axis)


def sigma(cond, fiber, direction):
    summed = jnp.zeros(fiber.shape, jnp.float32)
    for c in range(4):
        summed = jnp.where(fiber == c, cond[c, direction], summed)
    return summed


def cross_weight(sig, share, axis):
    place = lax.broadcasted_iota(jnp.int32, sig.shape, axis)
    inner = jnp.where(place < sig.shape[axis] - 1, HALF_STEP, 0.0)
    return inner * (sig + ahead(sig, axis)) * (share * ahead(share, axis))


def face_weight(sig_a, share_a, sig_b, share_b):
    return HALF_STEP * (sig_a + sig_b) * (share_a * share_b)


def cross(v, wx, wy):
    fx = wx * (ahead(v, 0) - v)
    fy = wy * (ahead(v, 1) - v)
    return (fx - behind(fx, 0)) + (fy - behind(fy, 1))


def reaction(v, g1, g2, g3):
    return 0.3 * (g1 * g2) * (1.0 - v) - 0.15 * g3 * v


def tanhs(v):
    return jnp.tanh(4.0 * v - 0.8), jnp.tanh(2.0 - 4.0 * v), jnp.tanh(4.0 * v - 3.2)


def gates_next(v, g1, g2, g3):
    t1, t2, t3 = tanhs(v)
    return (
        0.7 * g1 + (0.15 + 0.15 * t1),
        0.9 * g2 + (0.05 + 0.05 * t2),
        0.97 * g3 + (0.015 + 0.015 * t3),
    )


def fetch(copies, sems):
    started = [pltpu.make_async_copy(src, dst, sems.at[n]) for n, (src, dst) in enumerate(copies)]
    for copy in started:
        copy.start()
    for copy in started:
        copy.wait()


def edge_kernel(
    cond_in, flag, starts_in, tissue_in, fibers_in, pacing_in,
    up, down, up_tissue, down_tissue, starts, tissue, fibers, pacing, cond, sems,
):
    whole = pltpu.make_async_copy(starts_in.at[0], starts, sems.at[0])
    few = [
        pltpu.make_async_copy(src, dst, sems.at[n + 1])
        for n, (src, dst) in enumerate(
            ((cond_in, cond), (fibers_in, fibers), (tissue_in, tissue), (pacing_in, pacing))
        )
    ]
    for copy in few:
        copy.start()
    whole.start()
    for copy in few:
        copy.wait()
    ready = []
    for out_tissue, (b1, b2, b3, b4) in ((up_tissue, (7, 6, 5, 4)), (down_tissue, (0, 1, 2, 3))):
        share = [tissue[b].astype(jnp.float32) for b in (b1, b2, b3, b4)]
        sig0 = [sigma(cond, fibers[b], 0) for b in (b1, b2, b3, b4)]
        wz = [face_weight(sig0[i], share[i], sig0[i + 1], share[i + 1]) for i in range(3)]
        wx = [cross_weight(sigma(cond, fibers[b], 1), share[i], 0) for i, b in enumerate((b1, b2, b3))]
        wy = [cross_weight(sigma(cond, fibers[b], 2), share[i], 1) for i, b in enumerate((b1, b2, b3))]
        stim = [(0.6 * flag[0]) * pacing[b].astype(jnp.float32) for b in (b1, b2, b3)]
        out_tissue[FIB] = fibers[b1].astype(jnp.float32)
        out_tissue[TIS] = share[0]
        out_tissue[WIN] = wz[0]
        ready.append((wz, wx, wy, stim))
    whole.wait()
    for out, (b1, b2, b3, b4), (wz, wx, wy, stim) in zip((up, down), ((7, 6, 5, 4), (0, 1, 2, 3)), ready):
        v = [starts[0, b] for b in (b1, b2, b3, b4)]
        g = [[starts[n, b] for n in (1, 2, 3)] for b in (b1, b2, b3)]

        def own_step(i):
            total = v[i] + cross(v[i], wx[i], wy[i]) + reaction(v[i], *g[i]) + stim[i]
            total = total + wz[i] * (v[i + 1] - v[i])
            return total if i == 0 else total + wz[i - 1] * (v[i - 1] - v[i])

        out[V0] = v[0]
        out[P1] = own_step(0)
        gates = gates_next(v[0], *g[0])
        for n in range(3):
            out[G1 + n] = gates[n]
        v1_b2 = own_step(1)
        v1_b3 = own_step(2)
        out[Q2] = wz[0] * v1_b2 + stim[0]
        rest = v1_b2 + cross(v1_b2, wx[1], wy[1]) + reaction(v1_b2, *gates_next(v[1], *g[1])) + stim[1]
        rest = rest + wz[1] * (v1_b3 - v1_b2) - wz[0] * v1_b2
        out[Q3] = wz[0] * rest + stim[0]


class Fields:
    def __init__(self, inner, outer, rim_voltage, rim_gate):
        self.refs = (inner, outer)
        self.rims = (rim_voltage, rim_gate)

    def plane(self, field, layer):
        rim = self.rims[0] if field == 0 else self.rims[1]
        inside = rim <= layer < DEEP - rim
        return self.refs[0 if inside else 1][field, layer]

    def all(self, layer):
        return [self.plane(n, layer) for n in range(4)]


def forward_fields(starts, inner, outer):
    return [Fields(starts, None, 0, 0)] + [Fields(inner[j - 1], outer[j - 1], j, j - 1) for j in (1, 2, 3)]


def inner_layers(rim):
    return range(rim, DEEP - rim)


def rim_layers(rim):
    return [i for i in range(DEEP) if not rim <= i < DEEP - rim]


def rim_kernel(cond_in, tissue, fibers, low_tissue, high_tissue, rim, cond, sems):
    fetch([(cond_in, cond)], sems)
    for n, (beside, own) in enumerate(((low_tissue, 0), (high_tissue, DEEP - 1))):
        fib, tis = beside[FIB], beside[TIS]
        rim[n, C_W01] = face_weight(
            sigma(cond, fib, 0), tis, sigma(cond, fibers[own], 0), tissue[own].astype(jnp.float32)
        )
        rim[n, C_WIN] = beside[WIN]
        rim[n, C_WX] = cross_weight(sigma(cond, fib, 1), tis, 0)
        rim[n, C_WY] = cross_weight(sigma(cond, fib, 2), tis, 1)


def ahead_kernel(cond_in, flag, starts, tissue, fibers, pacing, wx, wy, wz, f1, f2, f3, f4, cond, sems):
    fetch([(cond_in, cond)], sems)
    before = None
    for i in range(DEEP):
        share = tissue[i].astype(jnp.float32)
        sig0 = sigma(cond, fibers[i], 0)
        wx[i] = cross_weight(sigma(cond, fibers[i], 1), share, 0)
        wy[i] = cross_weight(sigma(cond, fibers[i], 2), share, 1)
        if i:
            wz[i - 1] = face_weight(*before, sig0, share)
        before = (sig0, share)
    old = starts
    for step, new in enumerate((f1, f2, f3, f4)):
        below = None
        for i in inner_layers(step):
            v, *g = [old[n, i] for n in range(4)]
            for n, gate in enumerate(gates_next(v, *g)):
                new[n + 1, i] = gate
            if step == 0:
                low, high = i > 0, i < DEEP - 1
            else:
                low = high = step + 1 <= i < DEEP - step - 1
            if not (low or high):
                continue
            total = v + cross(v, wx[i], wy[i]) + reaction(v, *g)
            total = total + (0.6 * flag[0]) * pacing[i].astype(jnp.float32)
            if low:
                total = total - (wz[i - 1] * (v - old[0, i - 1]) if below is None else below)
            below = None
            if high:
                below = wz[i] * (old[0, i + 1] - v)
                total = total + below
            new[0, i] = total
        old = new


def forward_kernel(
    flag, starts, pacing, wx, wy, wz, rim, p1, p2, p3, p4, high, low,
    f1, f2, f3, f4, side,
):
    halo = []
    for n, (msg, own) in enumerate(((low, 0), (high, DEEP - 1))):
        inflow = rim[n, C_W01] * (msg[V0] - starts[0, own])
        f1[0, own] = p1[0, own] + inflow
        halo.append(msg[P1] - inflow)
        side[n, C_D1] = halo[n]
    fields = forward_fields(starts, (p1, p2, p3), (f1, f2, f3))
    for n in range(1, 4):
        for i in inner_layers(3):
            f4[n, i] = p4[n, i]
    for step in (1, 2, 3):
        old = fields[step]
        new = (f1, f2, f3, f4)[step]
        outflow = [None, None]
        above = None
        for i in rim_layers(step + 1):
            v, *g = old.all(i)
            if i not in inner_layers(step):
                for n, gate in enumerate(gates_next(v, *g)):
                    new[n + 1, i] = gate
            if i == 0:
                below = outflow[0] = rim[0, C_W01] * (v - halo[0])
            elif above is not None:
                below = above
            else:
                below = wz[i - 1] * (v - old.plane(0, i - 1))
            if i == DEEP - 1:
                above = rim[1, C_W01] * (halo[1] - v)
                outflow[1] = -above
            else:
                above = wz[i] * (old.plane(0, i + 1) - v)
            total = v + (above - below) + cross(v, wx[i], wy[i]) + reaction(v, *g)
            new[0, i] = total + (0.6 * flag[0]) * pacing[i].astype(jnp.float32)
            if i == step and step < 3:
                above = None
        if step == 3:
            continue
        for n, msg in enumerate((low, high)):
            v = halo[n]
            win = rim[n, C_WIN]
            g = [msg[G1], msg[G2], msg[G3]]
            if step == 1:
                extra = msg[Q2]
            else:
                v1 = side[n, C_D1]
                g1 = g
                g = gates_next(v1, *g1)
                extra = msg[Q3] + win * win * v1
                t1, t2, t3 = tanhs(v1)
                side[n, C_D2] = -0.3 * (g[0] * g[1]) - 0.15 * g[2]
                side[n, C_D1] = -0.3 * (g1[0] * g1[1]) - 0.15 * g1[2]
                side[n, C_E] = (
                    0.6 * (1.0 - t1 * t1) * (0.3 * g[1] * (1.0 - v))
                    - 0.2 * (1.0 - t2 * t2) * (0.3 * g[0] * (1.0 - v))
                    - 0.06 * (1.0 - t3 * t3) * (0.15 * v)
                )
            total = v + cross(v, rim[n, C_WX], rim[n, C_WY]) + reaction(v, *g)
            halo[n] = total + (extra - win * v) + outflow[n]


def pull_gates(a, f):
    av, a1, a2, a3 = a
    v, g1, g2, g3 = f
    rest = 0.3 * (1.0 - v) * av
    return 0.7 * a1 + g2 * rest, 0.9 * a2 + g1 * rest, 0.97 * a3 - 0.15 * v * av


def pull_voltage(a, f):
    av, a1, a2, a3 = a
    v, g1, g2, g3 = f
    t1, t2, t3 = tanhs(v)
    total = av * (1.0 - 0.3 * (g1 * g2) - 0.15 * g3)
    total = total + 0.6 * (1.0 - t1 * t1) * a1 - 0.2 * (1.0 - t2 * t2) * a2
    return total + 0.06 * (1.0 - t3 * t3) * a3


def send_kernel(ends, following, starts, p1, p2, p3, f1, f2, f3, wx, wy, wz, gap, up, down):
    fields = forward_fields(starts, (p1, p2, p3), (f1, f2, f3))
    for n in range(4):
        for i in range(DEEP):
            gap[n, i] = ends[n, i] - following[0, n, i]
    for out, (b1, sign) in ((up, (7, -1)), (down, (0, 1))):
        layers = [b1 + sign * d for d in range(4)]
        a = [[gap[n, b] for n in range(4)] for b in layers]
        out[0] = a[0][0]
        for m in range(3):
            fresh = []
            outer = None
            for d in range(3 - m):
                b = layers[d]
                f = fields[3 - m].all(b)
                face = wz[b - 1] if sign < 0 else wz[b]
                inner = face * (a[d + 1][0] - a[d][0])
                total = pull_voltage(a[d], f) + cross(a[d][0], wx[b], wy[b]) + inner
                if outer is not None:
                    total = total - outer
                fresh.append([total, *pull_gates(a[d], f)])
                outer = inner
            a = fresh
            out[m + 1] = a[0][0]


def back_kernel(gap, starts, p1, p2, p3, f1, f2, f3, wx, wy, wz, gate, a1, a2, a3, a4):
    fields = forward_fields(starts, (p1, p2, p3), (f1, f2, f3))
    old = gap
    for m, new in enumerate((a1, a2, a3, a4)):
        below = None
        for i in inner_layers(m):
            a = [old[n, i] for n in range(4)]
            f = fields[3 - m].all(i)
            for n, plane in enumerate(pull_gates(a, f)):
                new[n + 1, i] = plane
            if i not in inner_layers(m + 1):
                continue
            if below is None:
                below = wz[i - 1] * (a[0] - old[0, i - 1])
            above = wz[i] * (old[0, i + 1] - a[0])
            new[0, i] = pull_voltage(a, f) + (above - below) + cross(a[0], wx[i], wy[i])
            below = above
        old = new


def defect_kernel(starts, before, defect_out, defect, sems):
    copies = []
    for n in range(4):
        for i in range(DEEP):
            defect[n, i] = before[0, n, i] - starts[n, i]
        copies.append(pltpu.make_async_copy(defect.at[n], defect_out.at[0, n], sems.at[n]))
        copies[n].start()
    for copy in copies:
        copy.wait()


def pull_kernel(
    starts, gap, defect, p1, p2, p3, f1, f2, f3, b1, b2, b3, b4, wx, wy, wz, rim, side, low, high,
    gradient_out, work, gradient, sems,
):
    copies = []
    fields = forward_fields(starts, (p1, p2, p3), (f1, f2, f3))
    adjoints = [Fields(gap, None, 0, 0)] + [
        Fields(b, work.at[j], j + 1, j) for j, b in enumerate((b1, b2, b3))
    ]
    halo = [low[0], high[0]]
    first = [None, None]
    last = [None, None]
    for m in range(4):
        old = adjoints[m]
        outflow = [None, None]
        above = None
        for i in rim_layers(m + 1):
            a = old.all(i)
            f = fields[3 - m].all(i)
            if i == 0:
                below = outflow[0] = rim[0, C_W01] * (a[0] - halo[0])
            elif above is not None:
                below = above
            else:
                below = wz[i - 1] * (a[0] - old.plane(0, i - 1))
            if i == DEEP - 1:
                above = rim[1, C_W01] * (halo[1] - a[0])
                outflow[1] = -above
            else:
                above = wz[i] * (old.plane(0, i + 1) - a[0])
            fresh = [pull_voltage(a, f) + (above - below) + cross(a[0], wx[i], wy[i])]
            if i in inner_layers(m):
                if m == 3:
                    fresh += [b4[n, i] for n in (1, 2, 3)]
            else:
                fresh += pull_gates(a, f)
            if i == m and m < 3:
                above = None
            if m < 3:
                for n, plane in enumerate(fresh):
                    work[m, n, i] = plane
                continue
            for n, plane in enumerate(fresh):
                gradient[n, i] = plane - defect[n, i]
            copy = pltpu.make_async_copy(gradient.at[:, i], gradient_out.at[0, :, i], sems.at[i])
            copy.start()
            copies.append(copy)
        if m == 3:
            continue
        for n, msg in enumerate((low, high)):
            win, px, py = rim[n, C_WIN], rim[n, C_WX], rim[n, C_WY]
            if m == 0:
                change = first[n] = outflow[n]
            else:
                d = last[n]
                rate = side[n, C_D2] if m == 1 else side[n, C_D1]
                change = d + cross(d, px, py) + (rate - win) * d + outflow[n]
                if m == 2:
                    change = change + (win * win + side[n, C_E]) * first[n]
            halo[n] = msg[m + 1] + change
            last[n] = change
    for copy in copies:
        copy.wait()


VM = pl.BlockSpec(memory_space=pltpu.VMEM)
SM = pl.BlockSpec(memory_space=pltpu.SMEM)
ANY = pl.BlockSpec(memory_space=pl.ANY)
HBM = pl.BlockSpec(memory_space=pltpu.HBM)


def f32(*shape):
    return jax.ShapeDtypeStruct(shape, jnp.float32)


def i32(*shape):
    return jax.ShapeDtypeStruct(shape, jnp.int32)


def call(kernel, name, ins, outs, scratch=(), out_specs=None):
    return pl.pallas_call(
        kernel,
        name=name,
        in_specs=ins,
        out_specs=out_specs or [VM] * len(outs),
        out_shape=outs,
        scratch_shapes=list(scratch),
        compiler_params=pltpu.CompilerParams(vmem_limit_bytes=28 * 1024 * 1024),
    )


def nearest(sections, slabs, pairs):
    return [
        ((k ^ 2) * slabs + source, k * slabs + target) for k in range(sections) for source, target in pairs
    ]


def body(starts, tissue, fibers, pacing, conductances):
    plane = (NX, NY)
    slab = (DEEP, *plane)
    fields = f32(4, *slab)
    slabs = lax.axis_size("slab")
    sections = lax.axis_size("tm")
    upward = [(i, i + 1) for i in range(slabs - 1)]
    downward = [(i + 1, i) for i in range(slabs - 1)]
    earlier = [((i + 1) % sections, i) for i in range(sections)]
    later = [(i, (i + 1) % sections) for i in range(sections)]
    flag = (lax.axis_index("tm") == 0).astype(jnp.float32).reshape(1)

    conductances, starts, tissue, fibers, pacing = (
        pltpu.with_memory_space_constraint(arg, pltpu.HBM)
        for arg in (conductances, starts, tissue, fibers, pacing)
    )
    up, down, up_tissue, down_tissue, own, tis, fib, pac = call(
        edge_kernel,
        "edge",
        [HBM, SM] + [HBM] * 4,
        [f32(7, *plane)] * 2 + [f32(3, *plane)] * 2 + [fields] + [i32(*slab)] * 3,
        [pltpu.SMEM((4, 3), jnp.float32), pltpu.SemaphoreType.DMA((5,))],
    )(conductances, flag, starts, tissue, fibers, pacing)
    high = lax.ppermute(down, "slab", downward)
    low = lax.ppermute(up, "slab", upward)
    low_tissue = lax.ppermute(up_tissue, ("tm", "slab"), nearest(sections, slabs, upward))
    high_tissue = lax.ppermute(down_tissue, ("tm", "slab"), nearest(sections, slabs, downward))
    following = lax.ppermute(own[None], "tm", earlier)
    few = [pltpu.SMEM((4, 3), jnp.float32), pltpu.SemaphoreType.DMA((1,))]
    wx, wy, wz, p1, p2, p3, p4 = call(
        ahead_kernel,
        "ahead",
        [HBM, SM] + [VM] * 4,
        [f32(*slab), f32(*slab), f32(DEEP - 1, *plane)] + [fields] * 4,
        few,
    )(conductances, flag, own, tis, fib, pac)
    rim = call(rim_kernel, "rim", [HBM] + [VM] * 4, [f32(2, 4, *plane)], few)(
        conductances, tis, fib, low_tissue, high_tissue
    )[0]
    f1, f2, f3, ends, side = call(
        forward_kernel,
        "forward",
        [SM] + [VM] * 12,
        [fields] * 4 + [f32(2, 3, *plane)],
    )(flag, own, pac, wx, wy, wz, rim, p1, p2, p3, p4, high, low)
    before = lax.ppermute(ends[None], "tm", later)
    history = (own, p1, p2, p3, f1, f2, f3)
    gap, up, down = call(
        send_kernel, "send", [VM] * 12, [fields, f32(4, *plane), f32(4, *plane)]
    )(ends, following, *history, wx, wy, wz)
    low = lax.ppermute(up, "slab", upward)
    high = lax.ppermute(down, "slab", downward)
    inner = call(back_kernel, "back", [VM] * 11 + [ANY], [fields] * 4)(gap, *history, wx, wy, wz, up)
    defect, kept = call(
        defect_kernel,
        "defect",
        [VM] * 2,
        [f32(1, 4, *slab), fields],
        [pltpu.SemaphoreType.DMA((4,))],
        [ANY, VM],
    )(own, before)
    gradient = call(
        pull_kernel,
        "pull",
        [VM] * 20,
        [f32(1, 4, *slab)],
        [
            pltpu.VMEM((3, 4, *slab), jnp.float32),
            pltpu.VMEM((4, *slab), jnp.float32),
            pltpu.SemaphoreType.DMA((DEEP,)),
        ],
        [ANY],
    )(own, gap, kept, p1, p2, p3, f1, f2, f3, *inner, wx, wy, wz, rim, side, low, high)[0]
    return defect, gradient


def solution(mesh):
    spread = P("tm", None, "slab", None, None)
    placed = (spread, P("slab", None, None), P("slab", None, None), P("slab", None, None), P())
    return jax.shard_map(body, mesh=mesh, in_specs=placed, out_specs=(spread, spread), check_vma=False)
```
